256 devices in a mesh: front: 16 (over z, core), grid: 16 (over x, y).
Axes of the slice: x: 4, y: 4, z: 8, core: 2. Of those that a mesh axis runs over, the one named last changes fastest.
Arguments:
- child_blocks: bfloat16 [32, 3072, 3072], P('grid', 'front'), may hold values from -1.5 to 6, as said below
- orig_diag: bfloat16 [16, 1024, 1024], P('front', None, 'grid'), may hold values from -2.5 to 81, as said below
- orig_rows: bfloat16 [16, 1024, 6144], P('front', None, 'grid'), may hold values from -1.5 to 1.5
- child_map: int32 [32, 24], replicated, may hold values from 0 to 55, as said below
- child_parent: int32 [32], replicated, may hold values from 0 to 15, as said below
- pivot_order: int32 [16, 56], replicated, may hold values from 0 to 55, as said below
Outputs:
- upper_diag: float32 [16, 1024, 1024], P('front', None, 'grid')
- upper_rows: float32 [16, 1024, 6144], P('front', None, 'grid')
- schur: bfloat16 [16, 6144, 6144], P('front', None, 'grid')
The draws below stay inside these ranges and needn't reach their ends.
Inputs may be any that keep to these rules, and one draw needn't show every extreme that they name: `child_map`: each row names 24 different variable blocks. `child_parent`: every front is named by exactly two children. `pivot_order`: each row is a permutation of the front's variable blocks. `child_blocks`: each child's block is symmetric. `orig_diag`: each front's block is symmetric, and every pivot_block is positive definite.
All inputs are finite; a program needn't handle non-finite values.
Results may differ from the reference program's by a relative error of at most 0.001.
Values may be sent and summed in bfloat16 or wider, within the bound.
A program may use at most 128 MiB of HBM per device.

```python
import math
import jax
import jax.numpy as jnp
from jax import lax

ORDER = 7168
PANEL = 1024
CHILD = 3072
BLOCK = 128
TRAIL = 6144
FRONTS = 16
KIDS = 32


def symmetric_noise(child_key, order_size):
    raw_noise = jnp.clip(jax.random.normal(child_key, (order_size, order_size), jnp.float32), -4.0, 4.0)
    return (raw_noise + raw_noise.T) * (0.25 / math.sqrt(2.0))


def draw_child_blocks(key, part):

    def one_child(child_index):
        child_key = jax.random.fold_in(key, child_index)
        noise = symmetric_noise(child_key, CHILD)
        diag_level = jax.random.uniform(jax.random.fold_in(child_key, 11), (CHILD,), jnp.float32, 2.0, 6.0)
        identity = jnp.eye(CHILD, dtype=jnp.float32)
        return (noise * (1.0 - identity) + diag_level[:, None] * identity).astype(jnp.bfloat16)
    return lax.map(one_child, jnp.arange(KIDS, dtype=jnp.int32))


def draw_orig_diag(key, part):

    def one_front(front_index):
        front_key = jax.random.fold_in(key, front_index + 1000)
        noise = symmetric_noise(front_key, PANEL)
        diag_level = jnp.exp(jax.random.uniform(jax.random.fold_in(front_key, 13), (PANEL,), jnp.float32, math.log(40.0), math.log(80.0)))
        signs = jnp.where(jax.random.bernoulli(jax.random.fold_in(front_key, 17), 0.5, (PANEL,)), 1.0, -1.0).astype(jnp.float32)
        identity = jnp.eye(PANEL, dtype=jnp.float32)
        coupled = signs[:, None] * signs[None, :]
        return (noise * (1.0 - identity) + diag_level[:, None] * identity + coupled).astype(jnp.bfloat16)
    return lax.map(one_front, jnp.arange(FRONTS, dtype=jnp.int32))


def draw_child_map(key, part):
    key_list = jax.random.split(jax.random.fold_in(key, 21), KIDS)

    def one_map(map_key):
        return jax.random.permutation(map_key, ORDER // BLOCK)[:CHILD // BLOCK]
    return jax.vmap(one_map)(key_list).astype(jnp.int32)


def draw_child_parent(key, part):
    return (jax.random.permutation(jax.random.fold_in(key, 22), KIDS) // 2).astype(jnp.int32)


def draw_pivot_order(key, part):
    key_list = jax.random.split(jax.random.fold_in(key, 23), FRONTS)

    def one_order(order_key):
        return jax.random.permutation(order_key, ORDER // BLOCK)
    return jax.vmap(one_order)(key_list).astype(jnp.int32)


def shard_levels(own_key, dims, shards, low, high):
    def one(dim, blocks):
        draws = jax.random.uniform(jax.random.fold_in(jax.random.fold_in(own_key, 6), dim), (blocks,), jnp.float32, low / len(shards), high / len(shards))
        return jnp.repeat(jnp.exp(draws), dims[dim] // blocks).reshape((-1,) + (1,) * (len(dims) - dim - 1))

    level = one(*shards[0])
    for cut in shards[1:]:
        level = level * one(*cut)
    return level


def scatter_about(stream_key, dims, width, bound, pieces=(), held_as=jnp.bfloat16):
    entries = width * jax.random.normal(stream_key, dims, jnp.float32)
    if pieces:
        entries = entries * shard_levels(stream_key, dims, pieces, -0.22, 0.18)
    return jnp.clip(entries, -bound, bound).astype(held_as)


def setup_inputs(seed: int = 0) -> dict:
    streams_of = jax.random.split(jax.random.key(seed), 7)
    child_blocks = draw_child_blocks(jax.random.fold_in(streams_of[6], 71), 0)
    orig_diag = draw_orig_diag(jax.random.fold_in(streams_of[6], 71), 0)
    orig_rows = scatter_about(streams_of[2], (FRONTS, PANEL, TRAIL), 0.25, 1.5, ((0, 16), (2, 16)))
    child_map = draw_child_map(jax.random.fold_in(streams_of[6], 71), 0)
    child_parent = draw_child_parent(jax.random.fold_in(streams_of[6], 71), 0)
    pivot_order = draw_pivot_order(jax.random.fold_in(streams_of[6], 71), 0)
    return dict(child_blocks=child_blocks, orig_diag=orig_diag, orig_rows=orig_rows, child_map=child_map, child_parent=child_parent, pivot_order=pivot_order)


def child_order(child_parent):
    kid_total = child_parent.shape[0]
    kid_ids = jnp.arange(kid_total, dtype=jnp.int32)
    earlier = (child_parent[:, None] == child_parent[None, :]) & (kid_ids[None, :] < kid_ids[:, None])
    kid_rank = jnp.sum(earlier.astype(jnp.int32), axis=1).astype(jnp.int32)
    kid_slot = 2 * child_parent + kid_rank
    matches = kid_slot[None, :] == kid_ids[:, None]
    return jnp.sum(jnp.where(matches, kid_ids[None, :], 0), axis=1).astype(jnp.int32)

def child_positions(parents, maps, pivot_order):
    front_total = pivot_order.shape[0]
    front_blocks = pivot_order.shape[1]
    chosen = (parents[:, None] == jnp.arange(front_total, dtype=jnp.int32)[None, :]).astype(jnp.int32)
    piv_rows = jnp.sum(chosen[:, :, None] * pivot_order[None, :, :], axis=1).astype(jnp.int32)
    slot_ids = jnp.arange(front_blocks, dtype=jnp.int32)
    matches = piv_rows[:, None, :] == maps[:, :, None]
    return jnp.sum(jnp.where(matches, slot_ids[None, None, :], 0), axis=2).astype(jnp.int32)

def reference(child_blocks, orig_diag, orig_rows, child_map, child_parent, pivot_order):
    kid_order = child_order(child_parent)
    front_blocks = ORDER // BLOCK
    kid_blocks = CHILD // BLOCK

    def one_front(front_id):
        own_kids = lax.dynamic_slice_in_dim(kid_order, 2 * front_id, 2, 0)
        own_maps = jnp.take(child_map, own_kids, axis=0)
        own_parents = jnp.zeros((2,), jnp.int32) + front_id
        landing = child_positions(own_parents, own_maps, pivot_order)
        assembled = jnp.zeros((front_blocks, BLOCK, front_blocks, BLOCK), jnp.float32)
        for kid_rank in range(2):
            values = jnp.take(child_blocks, own_kids[kid_rank], axis=0).astype(jnp.float32)
            values = values.reshape(kid_blocks, BLOCK, kid_blocks, BLOCK).transpose(0, 2, 1, 3)
            spots = landing[kid_rank]
            assembled = assembled.at[spots[:, None], :, spots[None, :], :].add(values)
        assembled = assembled.reshape(ORDER, ORDER)
        pivot_block = assembled[:PANEL, :PANEL] + jnp.take(orig_diag, front_id, axis=0).astype(jnp.float32)
        panel_rows = assembled[:PANEL, PANEL:] + jnp.take(orig_rows, front_id, axis=0).astype(jnp.float32)
        trailing = assembled[PANEL:, PANEL:]
        lower_factor = jnp.linalg.cholesky(pivot_block)
        pivots = jnp.diagonal(lower_factor)
        upper_diag = pivots[:, None] * lower_factor.T
        solved = jax.scipy.linalg.solve_triangular(lower_factor, panel_rows, lower=True)
        upper_rows = pivots[:, None] * solved
        rounded = lax.optimization_barrier(solved.astype(jnp.bfloat16)).astype(jnp.float32)
        product = lax.dot_general(rounded.astype(jnp.float32), rounded.astype(jnp.float32), (((0,), (0,)), ((), ())), precision=lax.Precision.HIGHEST, preferred_element_type=jnp.float32)
        schur = (trailing - product).astype(jnp.bfloat16)
        return (upper_diag, upper_rows, schur)
    upper_diag, upper_rows, schur = lax.map(one_front, jnp.arange(FRONTS, dtype=jnp.int32))
    return (upper_diag, upper_rows, schur)
```

```python
import jax
import jax.numpy as jnp
from jax import lax
from jax.experimental import pallas as pl
from jax.experimental.pallas import tpu as pltpu
from jax.sharding import PartitionSpec as P

ORDER = 7168
PANEL = 1024
CHILD = 3072
BLOCK = 128
N = 1024
NB = 128
PC = 384
WT = N + PC
F32 = jnp.float32
BF = jnp.bfloat16


def split(x):
    hi=x.astype(BF); return hi,(x-hi.astype(F32)).astype(BF)
def dg(a,b,ca,cb):
    return lax.dot_general(a,b,(((ca,),(cb,)),((),())),preferred_element_type=F32)
def factor_block(m_ref, inv_ref):
    rid = lax.broadcasted_iota(jnp.int32,(8,1),0)
    G=[m_ref[8*g:8*g+8,:] for g in range(16)]
    B=lambda x:jnp.broadcast_to(x,(8,128))
    for q in range(16):
        c0=8*q
        Rb=[jnp.broadcast_to(G[q][s:s+1,:],(8,256)) for s in range(8)]
        E=[[B(Rb[s][:,c0+t:c0+t+1]) if t>=s else None for t in range(8)] for s in range(8)]
        inv=[None]*8
        for t in range(8):
            inv[t]=1.0/E[t][t]
            for s in range(t+1,8):
                m=E[t][s]*inv[t]
                for u in range(s,8): E[s][u]=E[s][u]-m*E[t][u]
                Rb[s]=Rb[s]-jnp.concatenate([m,m],1)*Rb[t]
        new=Rb[7]; iv=inv[7]
        for s in range(6,-1,-1):
            new=jnp.where(rid==s,Rb[s],new); iv=jnp.where(rid==s,inv[s],iv)
        m_ref[c0:c0+8,:]=new
        inv_ref[c0:c0+8,:]=iv
        if q<15:
            T=jnp.transpose(new[:,:128]*iv)
            for g in range(q+1,16):
                p=[T[8*g:8*g+8,t:t+1]*Rb[t] for t in range(8)]
                G[g]=G[g]-(((p[0]+p[1])+(p[2]+p[3]))+((p[4]+p[5])+(p[6]+p[7])))
def lu_kernel(a_ref,p_ref,ud_ref,ur_ref,s_ref,w,m_ref,inv_ref,uh,ul):
    g=lax.axis_index("grid")
    w[:,:N]=a_ref[...]; w[:,N:]=p_ref[...]
    eye=(lax.broadcasted_iota(jnp.int32,(NB,NB),0)==lax.broadcasted_iota(jnp.int32,(NB,NB),1)).astype(F32)
    def step(k,c):
        r0=pl.multiple_of(k*NB,NB)
        m_ref[:,:NB]=w[pl.ds(r0,NB),pl.ds(r0,NB)]
        m_ref[:,NB:]=eye
        factor_block(m_ref,inv_ref)
        lh,ll=split(m_ref[:,NB:])
        ah,al=split(w[pl.ds(r0,NB),:])
        u=dg(lh,ah,1,0)+(dg(lh,al,1,0)+dg(ll,ah,1,0))
        w[pl.ds(r0,NB),:]=u
        h,l=split(u); uh[...]=h; ul[...]=l
        iv=inv_ref[...]
        x=u[:,N:]
        ur_ref[pl.ds(r0,NB),:]=x
        rs=jnp.sqrt(iv)
        s_ref[pl.ds(r0,NB),:]=(x*jnp.concatenate([rs]*3,1)).astype(BF)
        def upd(i,c):
            i0=pl.multiple_of(i*NB,NB)
            xh,xl=split((uh[:,pl.ds(i0,NB)].astype(F32)+ul[:,pl.ds(i0,NB)].astype(F32))*iv)
            d=dg(xh,uh[...],0,0)+(dg(xh,ul[...],0,0)+dg(xl,uh[...],0,0))
            w[pl.ds(i0,NB),:]=w[pl.ds(i0,NB),:]-d
            return c
        lax.fori_loop(k+1,N//NB,upd,0)
        return c
    lax.fori_loop(0,N//NB,step,0)
    blk=pl.multiple_of((g//2)*NB,NB)
    x=w[:,pl.ds(blk,NB)]
    half=g%2
    x=jnp.where(half==1,x[:,64:],x[:,:64])
    col=64*g+lax.broadcasted_iota(jnp.int32,(N,64),1)
    ud_ref[...]=jnp.where(lax.broadcasted_iota(jnp.int32,(N,64),0)<=col,x,0.0)


def lu_call(a, p):
    vm = pl.BlockSpec(memory_space=pltpu.VMEM)
    return pl.pallas_call(
        lu_kernel,
        out_shape=(
            jax.ShapeDtypeStruct((N, 64), F32),
            jax.ShapeDtypeStruct((N, PC), F32),
            jax.ShapeDtypeStruct((N, PC), BF),
        ),
        in_specs=[vm, vm],
        out_specs=(vm, vm, vm),
        scratch_shapes=[
            pltpu.VMEM((N, WT), F32),
            pltpu.VMEM((NB, 2 * NB), F32),
            pltpu.VMEM((NB, NB), F32),
            pltpu.VMEM((NB, WT), BF),
            pltpu.VMEM((NB, WT), BF),
        ],
        compiler_params=pltpu.CompilerParams(vmem_limit_bytes=48 << 20),
    )(a, p)


def child_order(child_parent):
    kid_total = child_parent.shape[0]
    kid_ids = jnp.arange(kid_total, dtype=jnp.int32)
    earlier = (child_parent[:, None] == child_parent[None, :]) & (
        kid_ids[None, :] < kid_ids[:, None]
    )
    kid_rank = jnp.sum(earlier.astype(jnp.int32), axis=1)
    kid_slot = 2 * child_parent + kid_rank
    matches = kid_slot[None, :] == kid_ids[:, None]
    return jnp.sum(jnp.where(matches, kid_ids[None, :], 0), axis=1)


def child_positions(parents, maps, pivot_order):
    front_total = pivot_order.shape[0]
    front_blocks = pivot_order.shape[1]
    chosen = (parents[:, None] == jnp.arange(front_total, dtype=jnp.int32)[None, :]).astype(
        jnp.int32
    )
    piv_rows = jnp.sum(chosen[:, :, None] * pivot_order[None, :, :], axis=1)
    slot_ids = jnp.arange(front_blocks, dtype=jnp.int32)
    matches = piv_rows[:, None, :] == maps[:, :, None]
    return jnp.sum(jnp.where(matches, slot_ids[None, None, :], 0), axis=2)


def shards(child_blocks, orig_diag, orig_rows, child_map, child_parent, pivot_order):
    groups = lax.axis_size("grid")
    front_total = lax.axis_size("front")
    grid_index = lax.axis_index("grid")
    front_index = lax.axis_index("front")
    kid_count = child_blocks.shape[0]
    slab_rows = child_blocks.shape[1]
    front_blocks = ORDER // BLOCK
    kid_blocks = CHILD // BLOCK
    panel_blocks = PANEL // BLOCK
    sub_rows = BLOCK // 2
    panel_cols = orig_diag.shape[2]
    trail_cols = orig_rows.shape[2]
    kid_order = child_order(child_parent)
    first_kid = grid_index * kid_count
    parents = lax.dynamic_slice_in_dim(child_parent, first_kid, kid_count, 0)
    maps = lax.dynamic_slice_in_dim(child_map, first_kid, kid_count, 0)
    landing = child_positions(parents, maps, pivot_order)
    spread = (
        landing[:, :, None] == jnp.arange(front_blocks, dtype=jnp.int32)[None, None, :]
    ).astype(jnp.bfloat16)
    tiles = child_blocks.reshape(kid_count, slab_rows, kid_blocks, BLOCK)
    panel_send = jnp.einsum(
        "krab,kap->krpb", tiles, spread[:, :, :panel_blocks], preferred_element_type=jnp.float32
    ).astype(jnp.bfloat16)
    panel_send = panel_send.reshape(kid_count, slab_rows, groups, panel_cols)
    trail_send = jnp.einsum(
        "krab,kap->krpb", tiles, spread[:, :, panel_blocks:], preferred_element_type=jnp.float32
    ).astype(jnp.bfloat16)
    trail_send = trail_send.reshape(kid_count, slab_rows, groups, trail_cols)
    panel_part = lax.all_to_all(panel_send, "grid", split_axis=2, concat_axis=0, tiled=True)
    trail_part = lax.all_to_all(trail_send, "grid", split_axis=2, concat_axis=0, tiled=True)
    row_count = panel_part.shape[1]
    panel_sorted = jnp.take(panel_part, kid_order, axis=0).reshape(
        front_total, 2, row_count, 1, panel_cols
    )
    trail_sorted = jnp.take(trail_part, kid_order, axis=0).reshape(
        front_total, 2, row_count, 1, trail_cols
    )
    panel_in = lax.all_to_all(panel_sorted, "front", split_axis=0, concat_axis=0, tiled=True)
    trail_in = lax.all_to_all(trail_sorted, "front", split_axis=0, concat_axis=0, tiled=True)
    own_kids = lax.dynamic_slice_in_dim(kid_order, 2 * front_index, 2, 0)
    chosen = (own_kids[:, None] == jnp.arange(2 * front_total, dtype=jnp.int32)[None, :]).astype(
        jnp.int32
    )
    own_maps = jnp.sum(chosen[:, :, None] * child_map[None, :, :], axis=1)
    own_parents = jnp.zeros((2,), jnp.int32) + front_index
    own_landing = child_positions(own_parents, own_maps, pivot_order)
    sub_land = (
        2 * jnp.repeat(own_landing, 2, axis=1)
        + jnp.tile(jnp.arange(2, dtype=jnp.int32), kid_blocks)[None, :]
    )
    row_spread = (
        sub_land[:, :, None] == jnp.arange(ORDER // sub_rows, dtype=jnp.int32)[None, None, :]
    ).astype(jnp.bfloat16)
    row_spread = row_spread.reshape(2, front_total, slab_rows // sub_rows, ORDER // sub_rows)
    panel_rows_in = panel_in.reshape(front_total, 2, slab_rows // sub_rows, sub_rows, panel_cols)
    trail_rows_in = trail_in.reshape(front_total, 2, slab_rows // sub_rows, sub_rows, trail_cols)
    diag_sum = jnp.einsum(
        "ftuxw,tfup->pxw",
        panel_rows_in,
        row_spread[:, :, :, : PANEL // sub_rows],
        preferred_element_type=jnp.float32,
    ).reshape(PANEL, panel_cols)
    trail_sum = jnp.einsum(
        "ftuxw,tfup->pxw", trail_rows_in, row_spread, preferred_element_type=jnp.float32
    ).reshape(ORDER, trail_cols)
    pivot_whole = lax.all_gather(
        diag_sum + orig_diag[0].astype(jnp.float32), "grid", axis=1, tiled=True
    )
    panel_rows = trail_sum[:PANEL] + orig_rows[0].astype(jnp.float32)
    trailing = trail_sum[PANEL:]
    upper_diag, upper_rows, rounded = lu_call(pivot_whole, panel_rows)
    contract_rows = (((0,), (0,)), ((), ()))
    schur = (
        trailing
        - lax.dot_general(
            lax.all_gather(rounded, "grid", axis=1, tiled=True),
            rounded,
            contract_rows,
            preferred_element_type=jnp.float32,
        )
    ).astype(jnp.bfloat16)
    return (upper_diag[None], upper_rows[None], schur[None])


def solution(mesh):
    return jax.shard_map(
        shards,
        mesh=mesh,
        in_specs=(
            P("grid", "front", None),
            P("front", None, "grid"),
            P("front", None, "grid"),
            P(),
            P(),
            P(),
        ),
        out_specs=(P("front", None, "grid"), P("front", None, "grid"), P("front", None, "grid")),
        check_vma=False,
    )
```

```python
import functools

import jax
import jax.numpy as jnp
from jax import lax
from jax.experimental import pallas as pl
from jax.experimental.pallas import tpu as pltpu
from jax.sharding import PartitionSpec as P

N = 1024
NB = 128
PC = 384
WT = N + PC
SLOTS = 56
KB = 24
KIDS = 32
F32 = jnp.float32
BF = jnp.bfloat16
MESH = pl.DeviceIdType.MESH


def vm():
    return pl.BlockSpec(memory_space=pltpu.VMEM)


def sm():
    return pl.BlockSpec(memory_space=pltpu.SMEM)


def split(x):
    hi = x.astype(BF)
    return hi, (x - hi.astype(F32)).astype(BF)


def dg(a, b, ca, cb):
    return lax.dot_general(a, b, (((ca,), (cb,)), ((), ())), preferred_element_type=F32)


def kid_order_table(parent_ref, order, count):
    for p in range(KIDS // 2):
        count[p] = 0
    for c in range(KIDS):
        p = parent_ref[c]
        n = count[p]
        order[2 * p + n] = c
        count[p] = n + 1


def slot_table(child, parent, map_ref, piv_ref, tab, slots, base):
    for v in range(SLOTS):
        tab[v] = -1
    for a in range(KB):
        tab[map_ref[child, a]] = a
    for s in range(SLOTS):
        slots[base + s] = tab[piv_ref[parent, s]]


def pack_kernel(x_ref, map_ref, parent_ref, piv_ref, pan_ref, t0_ref, t1_ref, t2_ref, tab, slots):
    g = lax.axis_index("grid")
    for k in range(2):
        c = 2 * g + k
        slot_table(c, parent_ref[c], map_ref, piv_ref, tab, slots, k * SLOTS)
    lane = lax.broadcasted_iota(jnp.int32, (192, NB), 1)

    def block(k, slot):
        a = slots[k * SLOTS + slot]
        off = pl.multiple_of(jnp.maximum(a, 0) * NB, NB)
        x = x_ref[k, :, pl.ds(off, NB)]
        return jnp.where(a >= 0, x, jnp.zeros_like(x))

    def panel(j, carry):
        x0 = block(0, j).astype(F32)
        x1 = block(1, j).astype(F32)
        r0 = pltpu.roll(x0, 64, 1)
        r1 = pltpu.roll(x1, 64, 1)
        pan_ref[2 * j] = jnp.where(lane < 64, x0, r1).astype(BF)
        pan_ref[2 * j + 1] = jnp.where(lane < 64, r0, x1).astype(BF)
        return carry

    lax.fori_loop(0, 8, panel, 0)

    def trail(m, carry):
        for k in range(2):
            for i in range(3):
                x = block(k, 8 + 3 * m + i)
                for s, t_ref in enumerate((t0_ref, t1_ref, t2_ref)):
                    t_ref[m, k, :, i * NB : (i + 1) * NB] = x[64 * s : 64 * s + 64]
        return carry

    lax.fori_loop(0, 16, trail, 0)


def pack(x, child_map, child_parent, pivot_order):
    t = jax.ShapeDtypeStruct((16, 2, 64, PC), BF)
    return pl.pallas_call(
        pack_kernel,
        out_shape=(jax.ShapeDtypeStruct((16, 192, NB), BF), t, t, t),
        in_specs=[vm(), sm(), sm(), sm()],
        out_specs=(vm(), vm(), vm(), vm()),
        scratch_shapes=[pltpu.SMEM((SLOTS,), jnp.int32), pltpu.SMEM((2 * SLOTS,), jnp.int32)],
        compiler_params=pltpu.CompilerParams(vmem_limit_bytes=40 << 20),
        name="pack",
    )(x, child_map, child_parent, pivot_order)


def sort_panel_kernel(x_ref, parent_ref, o_ref, order, count):
    kid_order_table(parent_ref, order, count)
    lane = lax.broadcasted_iota(jnp.int32, (192, NB), 1)

    def one(p, carry):
        c0 = order[2 * p]
        c1 = order[2 * p + 1]
        x0 = x_ref[c0 // 2].astype(F32)
        x1 = x_ref[c1 // 2].astype(F32)
        x0 = jnp.where(c0 % 2 == 0, x0, pltpu.roll(x0, 64, 1))
        x1 = jnp.where(c1 % 2 == 1, x1, pltpu.roll(x1, 64, 1))
        o_ref[p] = jnp.where(lane < 64, x0, x1).astype(BF)
        return carry

    lax.fori_loop(0, 16, one, 0)


def sort_trail_kernel(x_ref, parent_ref, o_ref, order, count):
    kid_order_table(parent_ref, order, count)

    def one(p, carry):
        for t in range(2):
            c = order[2 * p + t]
            o_ref[p, t] = x_ref[c // 2, c % 2]
        return carry

    lax.fori_loop(0, 16, one, 0)


def sort_call(kernel, x, child_parent, name):
    return pl.pallas_call(
        kernel,
        out_shape=jax.ShapeDtypeStruct(x.shape, x.dtype),
        in_specs=[vm(), sm()],
        out_specs=vm(),
        scratch_shapes=[pltpu.SMEM((KIDS,), jnp.int32), pltpu.SMEM((KIDS // 2,), jnp.int32)],
        compiler_params=pltpu.CompilerParams(vmem_limit_bytes=20 << 20),
        name=name,
    )(x, child_parent)


def own_slots(parent_ref, map_ref, piv_ref, tab, slots, order, count):
    f = lax.axis_index("front")
    kid_order_table(parent_ref, order, count)
    for t in range(2):
        slot_table(order[2 * f + t], f, map_ref, piv_ref, tab, slots, t * SLOTS)


def rows_kernel(x_ref, od_ref, map_ref, parent_ref, piv_ref, d_ref, p_ref, tab, slots, order, count):
    own_slots(parent_ref, map_ref, piv_ref, tab, slots, order, count)

    def block(slot):
        halves = []
        for v in range(2):
            total = jnp.zeros((64, NB), F32)
            for t in range(2):
                a = slots[t * SLOTS + slot]
                u = 2 * jnp.maximum(a, 0) + v
                x = x_ref[u // 3, pl.ds(pl.multiple_of((u % 3) * 64, 64), 64), :].astype(F32)
                if t == 1:
                    x = pltpu.roll(x, 64, 1)
                total = total + jnp.where(a >= 0, x, 0.0)
            halves.append(total)
        return jnp.transpose(jnp.concatenate(halves, 0))[:64]

    for j in range(8):
        od = od_ref[0, j * NB : (j + 1) * NB, :].astype(F32)
        od = jnp.transpose(od)
        d_ref[:, j * NB : (j + 1) * NB] = block(j) + od

    def trail(m, carry):
        for i in range(3):
            p_ref[m, :, i * NB : (i + 1) * NB] = block(8 + 3 * m + i)
        return carry

    lax.fori_loop(0, 16, trail, 0)


def pivot_rows(x, orig_diag, child_map, child_parent, pivot_order):
    return pl.pallas_call(
        rows_kernel,
        out_shape=(
            jax.ShapeDtypeStruct((64, N), F32),
            jax.ShapeDtypeStruct((16, 64, PC), F32),
        ),
        in_specs=[vm(), vm(), sm(), sm(), sm()],
        out_specs=(vm(), vm()),
        scratch_shapes=[
            pltpu.SMEM((SLOTS,), jnp.int32),
            pltpu.SMEM((2 * SLOTS,), jnp.int32),
            pltpu.SMEM((KIDS,), jnp.int32),
            pltpu.SMEM((KIDS // 2,), jnp.int32),
        ],
        compiler_params=pltpu.CompilerParams(vmem_limit_bytes=20 << 20),
        name="pivot_rows",
    )(x, orig_diag, child_map, child_parent, pivot_order)


def factor_block(m_ref, inv_ref):
    rid = lax.broadcasted_iota(jnp.int32, (8, 1), 0)
    rows = [m_ref[8 * r : 8 * r + 8, :] for r in range(16)]
    for q in range(16):
        c0 = 8 * q
        rb = [jnp.broadcast_to(rows[q][s : s + 1, :], (8, 2 * NB)) for s in range(8)]
        e = [
            [
                jnp.broadcast_to(rb[s][:, c0 + t : c0 + t + 1], (8, NB)) if t >= s else None
                for t in range(8)
            ]
            for s in range(8)
        ]
        inv = [None] * 8
        for t in range(8):
            inv[t] = 1.0 / e[t][t]
            for s in range(t + 1, 8):
                m = e[t][s] * inv[t]
                for u in range(s, 8):
                    e[s][u] = e[s][u] - m * e[t][u]
                rb[s] = rb[s] - jnp.concatenate([m, m], 1) * rb[t]
        new, iv = rb[7], inv[7]
        for s in range(6, -1, -1):
            new = jnp.where(rid == s, rb[s], new)
            iv = jnp.where(rid == s, inv[s], iv)
        m_ref[c0 : c0 + 8, :] = new
        inv_ref[c0 : c0 + 8, :] = iv
        if q < 15:
            cols = jnp.transpose(new[:, :NB] * iv)
            for r in range(q + 1, 16):
                p = [cols[8 * r : 8 * r + 8, t : t + 1] * rb[t] for t in range(8)]
                rows[r] = rows[r] - (
                    ((p[0] + p[1]) + (p[2] + p[3])) + ((p[4] + p[5]) + (p[6] + p[7]))
                )


class Gather:
    def __init__(self, own, out, send, recv, rows):
        self.own, self.out, self.send, self.recv, self.half = own, out, send, recv, rows // 2
        self.f = lax.axis_index("front")
        g = lax.axis_index("grid")
        self.x, self.y = g // 4, g % 4

    def dev(self, axis, d):
        if axis == 0:
            return (self.f, lax.rem(self.x + d, 4) * 4 + self.y)
        return (self.f, self.x * 4 + lax.rem(self.y + d, 4))

    def at(self, axis, d, r0, rn):
        x, y = self.x, self.y
        if axis == 0:
            x = lax.rem(x + d, 4)
        else:
            y = lax.rem(y + d, 4)
        return self.out.at[x, y, pl.ds(r0, rn), :]

    def line(self, axis, d, r0, rn):
        if axis == 0:
            return self.out.at[lax.rem(self.x + d, 4), :, pl.ds(r0, rn), :]
        return self.out.at[:, lax.rem(self.y + d, 4), pl.ds(r0, rn), :]

    def copy(self, src, dst, sem, axis, d):
        return pltpu.make_async_remote_copy(
            src_ref=src,
            dst_ref=dst,
            send_sem=self.send.at[sem],
            recv_sem=self.recv.at[sem],
            device_id=self.dev(axis, d),
            device_id_type=MESH,
        )

    def stage(self, n):
        h = self.half
        q = h // 2
        out = []
        for axis in range(2):
            r0 = axis * h
            other = 1 - axis
            b = axis * 8 + 2 * n
            if n == 0:
                src = self.own.at[pl.ds(r0, h), :]
                out.append(self.copy(src, self.at(axis, 0, r0, h), b, axis, 1))
                out.append(self.copy(src, self.at(axis, 0, r0, h), b + 1, axis, 3))
            elif n == 1:
                a = self.at(axis, 3, r0, q)
                out.append(self.copy(a, a, b, axis, 1))
                a = self.at(axis, 1, r0 + q, q)
                out.append(self.copy(a, a, b + 1, axis, 3))
            elif n == 2:
                a = self.line(other, 0, r0, h)
                out.append(self.copy(a, a, b, other, 1))
                out.append(self.copy(a, a, b + 1, other, 3))
            else:
                a = self.line(other, 3, r0, q)
                out.append(self.copy(a, a, b, other, 1))
                a = self.line(other, 1, r0 + q, q)
                out.append(self.copy(a, a, b + 1, other, 3))
        return out

    def start(self, n):
        for c in self.stage(n):
            c.start()

    def wait_recv(self, n):
        for c in self.stage(n):
            c.wait_recv()

    def wait_send(self):
        for n in range(4):
            for c in self.stage(n):
                c.wait_send()


def lu_kernel(
    d_ref, p_ref, or_ref, ud_ref, ur_ref, s_ref, sg_ref,
    w, m_ref, inv_ref, uh, ul, st, dall, dsend, drecv, ssend, srecv, lsem,
):
    f = lax.axis_index("front")
    g = lax.axis_index("grid")
    x, y = g // 4, g % 4
    barrier = pltpu.get_barrier_semaphore()
    for dx, dy in ((1, 0), (3, 0), (0, 1), (0, 3)):
        other = lax.rem(x + dx, 4) * 4 + lax.rem(y + dy, 4)
        pl.semaphore_signal(barrier, inc=1, device_id=(f, other), device_id_type=MESH)
    pl.semaphore_wait(barrier, 4)
    gd = Gather(d_ref, dall, dsend, drecv, 64)
    gd.start(0)
    dall[x, y] = d_ref[...]
    w[:, N:] = p_ref[...] + or_ref[0].astype(F32)
    for n in range(3):
        gd.wait_recv(n)
        gd.start(n + 1)
    gd.wait_recv(3)
    gd.wait_send()
    for i in range(16):
        w[64 * i : 64 * i + 64, :N] = dall[i // 4, i % 4]
    eye = (
        lax.broadcasted_iota(jnp.int32, (NB, NB), 0) == lax.broadcasted_iota(jnp.int32, (NB, NB), 1)
    ).astype(F32)

    def gs(k):
        return Gather(st.at[k], sg_ref.at[k], ssend.at[k], srecv.at[k], PC)

    def local(k):
        return pltpu.make_async_copy(st.at[k], sg_ref.at[k, x, y], lsem.at[k])

    def move(k, n):
        c = gs(k)
        c.wait_recv(n - 1)
        if n == 2:
            local(k).wait()
        c.start(n)

    def step(k, carry):
        r0 = pl.multiple_of(k * NB, NB)
        m_ref[:, :NB] = w[pl.ds(r0, NB), pl.ds(r0, NB)]
        m_ref[:, NB:] = eye
        factor_block(m_ref, inv_ref)

        @pl.when(k >= 1)
        def _():
            move(k - 1, 1)

        @pl.when(k >= 2)
        def _():
            move(k - 2, 3)

        lh, ll = split(m_ref[:, NB:])
        ah, al = split(w[pl.ds(r0, NB), :])
        u = dg(lh, ah, 1, 0) + (dg(lh, al, 1, 0) + dg(ll, ah, 1, 0))
        w[pl.ds(r0, NB), :] = u
        h, l = split(u)
        uh[...] = h
        ul[...] = l
        iv = inv_ref[...]
        top = u[:, N:]
        ur_ref[pl.ds(r0, NB), :] = top
        rs = jnp.sqrt(iv)
        solved = top * jnp.concatenate([rs] * 3, 1)
        s_ref[pl.ds(r0, NB), :] = solved.astype(BF)
        st[k] = jnp.transpose(solved).astype(BF)
        gs(k).start(0)
        local(k).start()

        def upd(i, c):
            i0 = pl.multiple_of(i * NB, NB)
            xh, xl = split((uh[:, pl.ds(i0, NB)].astype(F32) + ul[:, pl.ds(i0, NB)].astype(F32)) * iv)
            d = dg(xh, uh[...], 0, 0) + (dg(xh, ul[...], 0, 0) + dg(xl, uh[...], 0, 0))
            w[pl.ds(i0, NB), :] = w[pl.ds(i0, NB), :] - d
            return c

        lax.fori_loop(k + 1, N // NB, upd, 0)

        @pl.when(k >= 1)
        def _():
            move(k - 1, 2)

        return carry

    last = N // NB - 1
    lax.fori_loop(0, N // NB, step, 0)
    move(last, 1)
    move(last - 1, 3)
    move(last, 2)
    blk = pl.multiple_of((g // 2) * NB, NB)
    own = w[:, pl.ds(blk, NB)]
    own = jnp.where(g % 2 == 1, own[:, 64:], own[:, :64])
    col = 64 * g + lax.broadcasted_iota(jnp.int32, (N, 64), 1)
    ud_ref[...] = jnp.where(lax.broadcasted_iota(jnp.int32, (N, 64), 0) <= col, own, 0.0)
    move(last, 3)

    def finish(k, carry):
        c = gs(k)
        c.wait_recv(3)
        c.wait_send()
        return carry

    lax.fori_loop(0, N // NB, finish, 0)


def lu_call(d, p, orig_rows):
    steps = N // NB
    return pl.pallas_call(
        lu_kernel,
        out_shape=(
            jax.ShapeDtypeStruct((N, 64), F32),
            jax.ShapeDtypeStruct((N, PC), F32),
            jax.ShapeDtypeStruct((N, PC), BF),
            jax.ShapeDtypeStruct((steps, 4, 4, PC, NB), BF),
        ),
        in_specs=[vm(), vm(), vm()],
        out_specs=(vm(), vm(), vm(), pl.BlockSpec(memory_space=pl.ANY)),
        scratch_shapes=[
            pltpu.VMEM((N, WT), F32),
            pltpu.VMEM((NB, 2 * NB), F32),
            pltpu.VMEM((NB, NB), F32),
            pltpu.VMEM((NB, WT), BF),
            pltpu.VMEM((NB, WT), BF),
            pltpu.VMEM((steps, PC, NB), BF),
            pltpu.VMEM((4, 4, 64, N), F32),
            pltpu.SemaphoreType.DMA((16,)),
            pltpu.SemaphoreType.DMA((16,)),
            pltpu.SemaphoreType.DMA((steps, 16)),
            pltpu.SemaphoreType.DMA((steps, 16)),
            pltpu.SemaphoreType.DMA((steps,)),
        ],
        compiler_params=pltpu.CompilerParams(
            vmem_limit_bytes=48 << 20, collective_id=0, has_side_effects=True
        ),
        cost_estimate=pl.CostEstimate(flops=3 * 10**9, bytes_accessed=300 * 10**6, transcendentals=0),
        name="factor_gather",
    )(d, p, orig_rows)


def schur_kernel(
    sg_ref, s_ref, t0_ref, t1_ref, t2_ref, map_ref, parent_ref, piv_ref, o_ref, tab, slots, order, count
):
    m = pl.program_id(0)

    @pl.when(m == 0)
    def _():
        own_slots(parent_ref, map_ref, piv_ref, tab, slots, order, count)

    lhs = jnp.concatenate([sg_ref[k, 0] for k in range(N // NB)], 1)
    prod = dg(lhs, s_ref[...], 1, 0)
    for i in range(3):
        for v in range(2):
            total = -prod[i * NB + v * 64 : i * NB + v * 64 + 64]
            for t in range(2):
                a = slots[t * SLOTS + 8 + 3 * m + i]
                u = 2 * jnp.maximum(a, 0) + v
                s = u % 3
                x = jnp.where(
                    s == 0, t0_ref[u // 3, t], jnp.where(s == 1, t1_ref[u // 3, t], t2_ref[u // 3, t])
                )
                total = total + jnp.where(a >= 0, x.astype(F32), 0.0)
            o_ref[0, i * NB + v * 64 : i * NB + v * 64 + 64, :] = total.astype(BF)


def schur_call(sg, s, t0, t1, t2, child_map, child_parent, pivot_order):
    steps = N // NB
    return pl.pallas_call(
        schur_kernel,
        out_shape=jax.ShapeDtypeStruct((1, 16 * PC, PC), BF),
        grid=(16,),
        in_specs=[
            pl.BlockSpec((steps, 1, PC, NB), lambda m: (0, m, 0, 0)),
            vm(), vm(), vm(), vm(), sm(), sm(), sm(),
        ],
        out_specs=pl.BlockSpec((1, PC, PC), lambda m: (0, m, 0)),
        scratch_shapes=[
            pltpu.SMEM((SLOTS,), jnp.int32),
            pltpu.SMEM((2 * SLOTS,), jnp.int32),
            pltpu.SMEM((KIDS,), jnp.int32),
            pltpu.SMEM((KIDS // 2,), jnp.int32),
        ],
        compiler_params=pltpu.CompilerParams(vmem_limit_bytes=40 << 20),
        name="schur",
    )(sg.reshape(steps, 16, PC, NB), s, t0, t1, t2, child_map, child_parent, pivot_order)


def exchange(x, axis):
    return lax.all_to_all(x, axis, split_axis=0, concat_axis=0, tiled=True)


def shards(child_blocks, orig_diag, orig_rows, child_map, child_parent, pivot_order):
    tables = (child_map, child_parent, pivot_order)
    panel, *trail = pack(child_blocks, *tables)
    panel = exchange(panel, "grid")
    trail = [exchange(t, "grid") for t in trail]
    panel = exchange(sort_call(sort_panel_kernel, panel, child_parent, "sort_panel"), "front")
    trail = [
        exchange(sort_call(sort_trail_kernel, t, child_parent, "sort_trail"), "front") for t in trail
    ]
    d, p = pivot_rows(panel, orig_diag, *tables)
    p = exchange(p, "grid").reshape(N, PC)
    upper_diag, upper_rows, s, sg = lu_call(d, p, orig_rows)
    schur = schur_call(sg, s, *trail, *tables)
    return upper_diag[None], upper_rows[None], schur


def solution(mesh):
    return jax.shard_map(
        shards,
        mesh=mesh,
        in_specs=(
            P("grid", "front", None),
            P("front", None, "grid"),
            P("front", None, "grid"),
            P(),
            P(),
            P(),
        ),
        out_specs=(P("front", None, "grid"), P("front", None, "grid"), P("front", None, "grid")),
        check_vma=False,
    )
```

```python
import functools

import jax
import jax.numpy as jnp
from jax import lax
from jax.experimental import pallas as pl
from jax.experimental.pallas import tpu as pltpu
from jax.sharding import PartitionSpec as P

N = 1024
NB = 128
PC = 384
WT = N + PC
SLOTS = 56
KB = 24
KIDS = 32
F32 = jnp.float32
BF = jnp.bfloat16
MESH = pl.DeviceIdType.MESH


def vm():
    return pl.BlockSpec(memory_space=pltpu.VMEM)


def sm():
    return pl.BlockSpec(memory_space=pltpu.SMEM)


def split(x):
    hi = x.astype(BF)
    return hi, (x - hi.astype(F32)).astype(BF)


def dg(a, b, ca, cb):
    return lax.dot_general(a, b, (((ca,), (cb,)), ((), ())), preferred_element_type=F32)


def kid_order_table(parent_ref, order, count):
    for p in range(KIDS // 2):
        count[p] = 0
    for c in range(KIDS):
        p = parent_ref[c]
        n = count[p]
        order[2 * p + n] = c
        count[p] = n + 1


def slot_table(child, parent, map_ref, piv_ref, tab, slots, base):
    for v in range(SLOTS):
        tab[v] = -1
    for a in range(KB):
        tab[map_ref[child, a]] = a
    for s in range(SLOTS):
        slots[base + s] = tab[piv_ref[parent, s]]


def own_slots(parent_ref, map_ref, piv_ref, tab, slots, order, count):
    f = lax.axis_index("front")
    kid_order_table(parent_ref, order, count)
    for t in range(2):
        slot_table(order[2 * f + t], f, map_ref, piv_ref, tab, slots, t * SLOTS)


def pack_kernel(
    x_ref, map_ref, parent_ref, piv_ref,
    pan_ref, t0_ref, t1_ref, t2_ref, order_ref, src_ref, odd_ref, front_ref, unit_ref, has_ref,
    tab, slots, count,
):
    g = lax.axis_index("grid")
    for k in range(2):
        c = 2 * g + k
        slot_table(c, parent_ref[c], map_ref, piv_ref, tab, slots, k * SLOTS)
    own_slots(parent_ref, map_ref, piv_ref, tab, front_ref, order_ref, count)
    for c in range(KIDS):
        src_ref[c] = order_ref[c] // 2
        odd_ref[c] = (order_ref[c] % 2).astype(F32)

    def units(s, carry):
        a = front_ref[s]
        for v in range(2):
            unit_ref[2 * s + v] = 2 * jnp.maximum(a, 0) + v
        has_ref[s] = (a >= 0).astype(F32)
        return carry

    lax.fori_loop(0, 2 * SLOTS, units, 0)
    lane = lax.broadcasted_iota(jnp.int32, (192, NB), 1)

    def block(k, slot):
        a = slots[k * SLOTS + slot]
        off = pl.multiple_of(jnp.maximum(a, 0) * NB, NB)
        x = x_ref[k, :, pl.ds(off, NB)]
        return jnp.where(a >= 0, x, jnp.zeros_like(x))

    def panel(j, carry):
        x0 = block(0, j).astype(F32)
        x1 = block(1, j).astype(F32)
        r0 = pltpu.roll(x0, 64, 1)
        r1 = pltpu.roll(x1, 64, 1)
        pan_ref[2 * j] = jnp.where(lane < 64, x0, r1).astype(BF)
        pan_ref[2 * j + 1] = jnp.where(lane < 64, r0, x1).astype(BF)
        return carry

    lax.fori_loop(0, 8, panel, 0)

    def trail(m, carry):
        for k in range(2):
            for i in range(3):
                x = block(k, 8 + 3 * m + i)
                for s, t_ref in enumerate((t0_ref, t1_ref, t2_ref)):
                    t_ref[m, k, :, i * NB : (i + 1) * NB] = x[64 * s : 64 * s + 64]
        return carry

    lax.fori_loop(0, 16, trail, 0)


def pack(x, child_map, child_parent, pivot_order):
    t = jax.ShapeDtypeStruct((16, 2, 64, PC), BF)
    ints = lambda n: jax.ShapeDtypeStruct((n,), jnp.int32)
    floats = lambda n: jax.ShapeDtypeStruct((n,), F32)
    return pl.pallas_call(
        pack_kernel,
        out_shape=(
            jax.ShapeDtypeStruct((16, 192, NB), BF), t, t, t,
            ints(KIDS), ints(KIDS), floats(KIDS), ints(2 * SLOTS), ints(4 * SLOTS), floats(2 * SLOTS),
        ),
        in_specs=[vm(), sm(), sm(), sm()],
        out_specs=(vm(), vm(), vm(), vm(), sm(), sm(), sm(), sm(), sm(), sm()),
        scratch_shapes=[
            pltpu.SMEM((SLOTS,), jnp.int32),
            pltpu.SMEM((2 * SLOTS,), jnp.int32),
            pltpu.SMEM((KIDS // 2,), jnp.int32),
        ],
        compiler_params=pltpu.CompilerParams(vmem_limit_bytes=24 << 20),
        name="pack",
    )(x, child_map, child_parent, pivot_order)


def factor_block(m_ref, inv_ref, hook):
    rid = lax.broadcasted_iota(jnp.int32, (8, 1), 0)
    rows = [m_ref[8 * r : 8 * r + 8, :] for r in range(16)]
    for q in range(16):
        if q == 8:
            hook()
        c0 = 8 * q
        rb = [jnp.broadcast_to(rows[q][s : s + 1, :], (8, 2 * NB)) for s in range(8)]
        e = [
            [
                jnp.broadcast_to(rb[s][:, c0 + t : c0 + t + 1], (8, NB)) if t >= s else None
                for t in range(8)
            ]
            for s in range(8)
        ]
        inv = [None] * 8
        for t in range(8):
            inv[t] = 1.0 / e[t][t]
            for s in range(t + 1, 8):
                m = e[t][s] * inv[t]
                for u in range(s, 8):
                    e[s][u] = e[s][u] - m * e[t][u]
                rb[s] = rb[s] - jnp.concatenate([m, m], 1) * rb[t]
        new, iv = rb[7], inv[7]
        for s in range(6, -1, -1):
            new = jnp.where(rid == s, rb[s], new)
            iv = jnp.where(rid == s, inv[s], iv)
        m_ref[c0 : c0 + 8, :] = new
        inv_ref[c0 : c0 + 8, :] = iv
        if q < 15:
            cols = jnp.transpose(new[:, :NB] * iv)
            for r in range(q + 1, 16):
                p = [cols[8 * r : 8 * r + 8, t : t + 1] * rb[t] for t in range(8)]
                rows[r] = rows[r] - (
                    ((p[0] + p[1]) + (p[2] + p[3])) + ((p[4] + p[5]) + (p[6] + p[7]))
                )


class Gather:
    def __init__(self, own, out, send, recv, rows):
        self.own, self.out, self.send, self.recv, self.half = own, out, send, recv, rows // 2
        self.f = lax.axis_index("front")
        g = lax.axis_index("grid")
        self.x, self.y = g // 4, g % 4

    def dev(self, axis, d):
        if axis == 0:
            return (self.f, lax.rem(self.x + d, 4) * 4 + self.y)
        return (self.f, self.x * 4 + lax.rem(self.y + d, 4))

    def at(self, axis, d, r0, rn):
        x, y = self.x, self.y
        if axis == 0:
            x = lax.rem(x + d, 4)
        else:
            y = lax.rem(y + d, 4)
        return self.out.at[x, y, pl.ds(r0, rn), :]

    def line(self, axis, d, r0, rn):
        if axis == 0:
            return self.out.at[lax.rem(self.x + d, 4), :, pl.ds(r0, rn), :]
        return self.out.at[:, lax.rem(self.y + d, 4), pl.ds(r0, rn), :]

    def copy(self, src, dst, sem, axis, d):
        return pltpu.make_async_remote_copy(
            src_ref=src,
            dst_ref=dst,
            send_sem=self.send.at[sem],
            recv_sem=self.recv.at[sem],
            device_id=self.dev(axis, d),
            device_id_type=MESH,
        )

    def stage(self, n):
        h = self.half
        q = h // 2
        out = []
        for axis in range(2):
            r0 = axis * h
            other = 1 - axis
            b = axis * 8
            if n == 0:
                src = self.own.at[pl.ds(r0, h), :]
                for i, d in enumerate((1, 3, 2)):
                    out.append(self.copy(src, self.at(axis, 0, r0, h), b + i, axis, d))
            elif n == 1:
                a = self.line(other, 0, r0, h)
                out.append(self.copy(a, a, b + 3, other, 1))
                out.append(self.copy(a, a, b + 4, other, 3))
            else:
                a = self.line(other, 3, r0, q)
                out.append(self.copy(a, a, b + 5, other, 1))
                a = self.line(other, 1, r0 + q, q)
                out.append(self.copy(a, a, b + 6, other, 3))
        return out

    def start(self, n):
        for c in self.stage(n):
            c.start()

    def wait_recv(self, n):
        for c in self.stage(n):
            c.wait_recv()

    def wait_send(self):
        for n in range(3):
            for c in self.stage(n):
                c.wait_send()


class Swap:
    def __init__(self, axis, src, dst, send, recv, local):
        f, g = lax.axis_index("front"), lax.axis_index("grid")
        self.axis, self.f, self.g = axis, f, g
        self.me = g if axis == "grid" else f
        self.src, self.dst, self.send, self.recv, self.local = src, dst, send, recv, local

    def copy(self, i):
        if self.axis == "grid":
            to = lax.rem(self.g // 4 + i // 4, 4) * 4 + lax.rem(self.g % 4 + i % 4, 4)
            dev = (self.f, to)
        else:
            to = lax.rem(self.f // 2 + i // 2, 8) * 2 + lax.rem(self.f % 2 + i % 2, 2)
            dev = (to, self.g)
        return pltpu.make_async_remote_copy(
            src_ref=self.src.at[to],
            dst_ref=self.dst(self.me),
            send_sem=self.send.at[i],
            recv_sem=self.recv.at[i],
            device_id=dev,
            device_id_type=MESH,
        )

    def keep(self):
        return pltpu.make_async_copy(self.src.at[self.me], self.dst(self.me), self.local)

    def start(self):
        def one(i, c):
            self.copy(i).start()
            return c

        lax.fori_loop(1, 16, one, 0)
        self.keep().start()

    def wait_recv(self):
        def one(i, c):
            self.copy(i).wait_recv()
            return c

        lax.fori_loop(1, 16, one, 0)
        self.keep().wait()

    def wait_send(self):
        def one(i, c):
            self.copy(i).wait_send()
            return c

        lax.fori_loop(1, 16, one, 0)


def main_kernel(
    ps1, a0, a1, a2, od_ref, or_ref, order, src_tab, odd, unit, has,
    ud_ref, ur_ref, s_ref, sg_ref, o0_ref, o1_ref, o2_ref,
    pr1, ps2, pr2, b0, b1, b2, c0, c1, c2, dsnd, psnd, prcv,
    w, m_ref, inv_ref, uh, ul, st, dall,
    asend, arecv, dsend, drecv, ssend, srecv, lsem, ksem,
):
    f = lax.axis_index("front")
    g = lax.axis_index("grid")
    x, y = g // 4, g % 4
    barrier = pltpu.get_barrier_semaphore()

    def greet(i, c):
        to = lax.rem(g + i, 16)
        pl.semaphore_signal(barrier, inc=1, device_id=(f, to), device_id_type=MESH)
        to = lax.rem(f + i, 16)
        pl.semaphore_signal(barrier, inc=1, device_id=(to, g), device_id_type=MESH)
        return c

    lax.fori_loop(1, 16, greet, 0)

    def swap(n, axis, src, dst):
        return Swap(axis, src, dst, asend.at[n], arecv.at[n], ksem.at[n])

    lane = lax.broadcasted_iota(jnp.int32, (192, NB), 1)

    panel1 = swap(0, "grid", ps1, lambda me: pr1.at[me])
    panel2 = swap(1, "front", ps2, lambda me: pr2.at[pl.ds(3 * me, 3)])
    pswap = swap(2, "grid", psnd, lambda me: prcv.at[pl.ds(64 * me, 64), :])

    def trail1(s):
        dst = (b0, b1, b2)[s]
        return swap(3 + s, "grid", (a0, a1, a2)[s], lambda me: dst.at[pl.ds(2 * me, 2)])

    def trail2(s):
        dst = (o0_ref, o1_ref, o2_ref)[s]
        return swap(6 + s, "front", (c0, c1, c2)[s], lambda me: dst.at[me])

    pl.semaphore_wait(barrier, 30)
    panel1.start()

    trail1(0).start()
    trail1(1).start()
    panel1.wait_recv()

    def sort_panel(p, carry):
        x0 = pr1[src_tab[2 * p]].astype(F32)
        x1 = pr1[src_tab[2 * p + 1]].astype(F32)
        m0 = odd[2 * p]
        m1 = odd[2 * p + 1]
        x0 = x0 * (1.0 - m0) + pltpu.roll(x0, 64, 1) * m0
        x1 = x1 * m1 + pltpu.roll(x1, 64, 1) * (1.0 - m1)
        z = jnp.where(lane < 64, x0, x1).astype(BF)
        for v in range(3):
            ps2[p, v] = z[64 * v : 64 * v + 64]
        return carry

    lax.fori_loop(0, 16, sort_panel, 0)
    panel2.start()

    def sort_trail(s):
        trail1(s).wait_recv()
        src, dst = (b0, b1, b2)[s], (c0, c1, c2)[s]

        def one(p, carry):
            for t in range(2):
                dst[p, t] = src[order[2 * p + t]]
            return carry

        lax.fori_loop(0, 16, one, 0)
        trail2(s).start()

    sort_trail(0)
    panel2.wait_recv()

    def pivot_rows(slot):
        halves = []
        for v in range(2):
            total = jnp.zeros((64, NB), F32)
            for t in range(2):
                z = pr2[unit[2 * (t * SLOTS + slot) + v]].astype(F32)
                if t == 1:
                    z = pltpu.roll(z, 64, 1)
                total = total + z * has[t * SLOTS + slot]
            halves.append(total)
        return jnp.transpose(jnp.concatenate(halves, 0))[:64]

    for j in range(8):
        od = jnp.transpose(od_ref[0, j * NB : (j + 1) * NB, :].astype(F32))
        dsnd[:, j * NB : (j + 1) * NB] = pivot_rows(j) + od
    gd = Gather(dsnd, dall, dsend, drecv, 64)
    gd.start(0)
    dall[x, y] = dsnd[...]

    def rest(m, carry):
        for i in range(3):
            psnd[m, :, i * NB : (i + 1) * NB] = pivot_rows(8 + 3 * m + i)
        return carry

    lax.fori_loop(0, 16, rest, 0)
    for n in range(2):
        gd.wait_recv(n)
        gd.start(n + 1)
    pswap.start()
    trail1(2).start()
    sort_trail(1)
    gd.wait_recv(2)
    for i in range(16):
        w[64 * i : 64 * i + 64, :N] = dall[i // 4, i % 4]
    eye = (
        lax.broadcasted_iota(jnp.int32, (NB, NB), 0) == lax.broadcasted_iota(jnp.int32, (NB, NB), 1)
    ).astype(F32)

    def gs(k):
        return Gather(st.at[k], sg_ref.at[k], ssend.at[k], srecv.at[k], PC)

    def local(k):
        return pltpu.make_async_copy(st.at[k], sg_ref.at[k, x, y], lsem.at[k])

    def move(k, n):
        c = gs(k)
        c.wait_recv(n - 1)
        if n == 1:
            local(k).wait()
        c.start(n)

    def step(k, carry):
        r0 = pl.multiple_of(k * NB, NB)
        m_ref[:, :NB] = w[pl.ds(r0, NB), pl.ds(r0, NB)]
        m_ref[:, NB:] = eye

        def hook():
            @pl.when(k >= 1)
            def _():
                move(k - 1, 1)

        factor_block(m_ref, inv_ref, hook)

        @pl.when(k == 0)
        def _():
            pswap.wait_recv()
            w[:, N:] = prcv[...] + or_ref[0].astype(F32)

        @pl.when(k == 2)
        def _():
            sort_trail(2)

        lh, ll = split(m_ref[:, NB:])
        ah, al = split(w[pl.ds(r0, NB), :])
        u = dg(lh, ah, 1, 0) + (dg(lh, al, 1, 0) + dg(ll, ah, 1, 0))
        w[pl.ds(r0, NB), :] = u
        h, l = split(u)
        uh[...] = h
        ul[...] = l
        iv = inv_ref[...]
        top = u[:, N:]
        ur_ref[pl.ds(r0, NB), :] = top
        rs = jnp.sqrt(iv)
        solved = top * jnp.concatenate([rs] * 3, 1)
        s_ref[pl.ds(r0, NB), :] = solved.astype(BF)
        st[k] = jnp.transpose(solved).astype(BF)
        gs(k).start(0)
        local(k).start()

        def upd(i, c):
            i0 = pl.multiple_of(i * NB, NB)
            xh, xl = split((uh[:, pl.ds(i0, NB)].astype(F32) + ul[:, pl.ds(i0, NB)].astype(F32)) * iv)
            d = dg(xh, uh[...], 0, 0) + (dg(xh, ul[...], 0, 0) + dg(xl, uh[...], 0, 0))
            w[pl.ds(i0, NB), :] = w[pl.ds(i0, NB), :] - d
            return c

        lax.fori_loop(k + 1, N // NB, upd, 0)

        @pl.when(k >= 1)
        def _():
            move(k - 1, 2)

        return carry

    last = N // NB - 1
    lax.fori_loop(0, N // NB, step, 0)
    move(last, 1)
    blk = pl.multiple_of((g // 2) * NB, NB)
    own = w[:, pl.ds(blk, NB)]
    own = jnp.where(g % 2 == 1, own[:, 64:], own[:, :64])
    col = 64 * g + lax.broadcasted_iota(jnp.int32, (N, 64), 1)
    ud_ref[...] = jnp.where(lax.broadcasted_iota(jnp.int32, (N, 64), 0) <= col, own, 0.0)
    move(last, 2)
    for s in range(3):
        trail1(s).wait_send()
        trail2(s).wait_send()
        trail2(s).wait_recv()
    for e in (panel1, panel2, pswap):
        e.wait_send()
    gd.wait_send()

    def finish(k, carry):
        c = gs(k)
        c.wait_recv(2)
        c.wait_send()
        return carry

    lax.fori_loop(0, N // NB, finish, 0)


def main_call(ps1, a0, a1, a2, orig_diag, orig_rows, *tables):
    steps = N // NB
    hbm = pl.BlockSpec(memory_space=pl.ANY)
    out = jax.ShapeDtypeStruct((16, 2, 64, PC), BF)
    panel = pltpu.VMEM((16, 192, NB), BF)
    send = pltpu.VMEM((16, 2, 64, PC), BF)
    recv = pltpu.VMEM((KIDS, 64, PC), BF)
    sems = pltpu.SemaphoreType.DMA
    return pl.pallas_call(
        main_kernel,
        out_shape=(
            jax.ShapeDtypeStruct((N, 64), F32),
            jax.ShapeDtypeStruct((N, PC), F32),
            jax.ShapeDtypeStruct((N, PC), BF),
            jax.ShapeDtypeStruct((steps, 4, 4, PC, NB), BF),
            out, out, out,
        ),
        in_specs=[hbm, hbm, hbm, hbm, vm(), vm(), sm(), sm(), sm(), sm(), sm()],
        out_specs=(vm(), vm(), vm(), hbm, hbm, hbm, hbm),
        scratch_shapes=[
            panel, pltpu.VMEM((16, 3, 64, NB), BF), pltpu.VMEM((48, 64, NB), BF),
            recv, recv, recv, send, send, send,
            pltpu.VMEM((64, N), F32),
            pltpu.VMEM((16, 64, PC), F32),
            pltpu.VMEM((N, PC), F32),
            pltpu.VMEM((N, WT), F32),
            pltpu.VMEM((NB, 2 * NB), F32),
            pltpu.VMEM((NB, NB), F32),
            pltpu.VMEM((NB, WT), BF),
            pltpu.VMEM((NB, WT), BF),
            pltpu.VMEM((steps, PC, NB), BF),
            pltpu.VMEM((4, 4, 64, N), F32),
            sems((9, 16)), sems((9, 16)), sems((16,)), sems((16,)),
            sems((steps, 16)), sems((steps, 16)), sems((steps,)), sems((9,)),
        ],
        compiler_params=pltpu.CompilerParams(
            vmem_limit_bytes=56 << 20, collective_id=0, has_side_effects=True
        ),
        name="assemble_factor_gather",
    )(ps1, a0, a1, a2, orig_diag, orig_rows, *tables)


def schur_kernel(
    sg_ref, s_ref, t0_ref, t1_ref, t2_ref, slots, o_ref
):
    m = pl.program_id(0)

    lhs = jnp.concatenate([sg_ref[k, 0] for k in range(N // NB)], 1)
    prod = dg(lhs, s_ref[...], 1, 0)
    for i in range(3):
        for v in range(2):
            total = -prod[i * NB + v * 64 : i * NB + v * 64 + 64]
            for t in range(2):
                a = slots[t * SLOTS + 8 + 3 * m + i]
                u = 2 * jnp.maximum(a, 0) + v
                s = u % 3
                x = jnp.where(
                    s == 0, t0_ref[u // 3, t], jnp.where(s == 1, t1_ref[u // 3, t], t2_ref[u // 3, t])
                )
                total = total + jnp.where(a >= 0, x.astype(F32), 0.0)
            o_ref[0, i * NB + v * 64 : i * NB + v * 64 + 64, :] = total.astype(BF)


def schur_call(sg, s, t0, t1, t2, front):
    steps = N // NB
    return pl.pallas_call(
        schur_kernel,
        out_shape=jax.ShapeDtypeStruct((1, 16 * PC, PC), BF),
        grid=(16,),
        in_specs=[
            pl.BlockSpec((steps, 1, PC, NB), lambda m: (0, m, 0, 0)),
            vm(), vm(), vm(), vm(), sm(),
        ],
        out_specs=pl.BlockSpec((1, PC, PC), lambda m: (0, m, 0)),
        compiler_params=pltpu.CompilerParams(vmem_limit_bytes=40 << 20),
        name="schur",
    )(sg.reshape(steps, 16, PC, NB), s, t0, t1, t2, front)


def shards(child_blocks, orig_diag, orig_rows, child_map, child_parent, pivot_order):
    panel, a0, a1, a2, order, src, odd, front, unit, has = pack(
        child_blocks, child_map, child_parent, pivot_order
    )
    upper_diag, upper_rows, s, sg, *trail = main_call(
        panel, a0, a1, a2, orig_diag, orig_rows, order, src, odd, unit, has
    )
    schur = schur_call(sg, s, *trail, front)
    return upper_diag[None], upper_rows[None], schur


def solution(mesh):
    return jax.shard_map(
        shards,
        mesh=mesh,
        in_specs=(
            P("grid", "front", None),
            P("front", None, "grid"),
            P("front", None, "grid"),
            P(),
            P(),
            P(),
        ),
        out_specs=(P("front", None, "grid"), P("front", None, "grid"), P("front", None, "grid")),
        check_vma=False,
    )
```

```python
import functools

import jax
import jax.numpy as jnp
from jax import lax
from jax.experimental import pallas as pl
from jax.experimental.pallas import tpu as pltpu
from jax.sharding import PartitionSpec as P

N = 1024
NB = 128
PC = 384
WT = N + PC
SLOTS = 56
KB = 24
KIDS = 32
ORDER = 0
SOURCE = ORDER + KIDS
UNIT = SOURCE + KIDS
FRONT = UNIT + 4 * SLOTS
INTS = FRONT + 2 * SLOTS
HAS = KIDS
FLOATS = HAS + 2 * SLOTS
PW = 5 * NB
F32 = jnp.float32
BF = jnp.bfloat16
MESH = pl.DeviceIdType.MESH


def vm():
    return pl.BlockSpec(memory_space=pltpu.VMEM)


def sm():
    return pl.BlockSpec(memory_space=pltpu.SMEM)


def split(x):
    hi = x.astype(BF)
    return hi, (x - hi.astype(F32)).astype(BF)


def dg(a, b, ca, cb):
    return lax.dot_general(a, b, (((ca,), (cb,)), ((), ())), preferred_element_type=F32)


def kid_order_table(parent_ref, order, count):
    for p in range(KIDS // 2):
        count[p] = 0
    for c in range(KIDS):
        p = parent_ref[c]
        n = count[p]
        order[2 * p + n] = c
        count[p] = n + 1


def slot_table(child, parent, map_ref, piv_ref, tab, slots, base):
    for v in range(SLOTS):
        tab[v] = -1
    for a in range(KB):
        tab[map_ref[child, a]] = a
    for s in range(SLOTS):
        slots[base + s] = tab[piv_ref[parent, s]]


def own_slots(parent_ref, map_ref, piv_ref, tab, slots, order, count):
    f = lax.axis_index("front")
    kid_order_table(parent_ref, order, count)
    for t in range(2):
        slot_table(order[2 * f + t], f, map_ref, piv_ref, tab, slots, t * SLOTS)


def pack_kernel(
    x_ref, map_ref, parent_ref, piv_ref,
    pan_ref, t0_ref, t1_ref, t2_ref, int_ref, float_ref,
    tab, slots, count, order_ref, front_ref,
):
    g = lax.axis_index("grid")
    for k in range(2):
        c = 2 * g + k
        slot_table(c, parent_ref[c], map_ref, piv_ref, tab, slots, k * SLOTS)
    own_slots(parent_ref, map_ref, piv_ref, tab, front_ref, order_ref, count)
    for c in range(KIDS):
        int_ref[ORDER + c] = order_ref[c]
        int_ref[SOURCE + c] = order_ref[c] // 2
        float_ref[c] = (order_ref[c] % 2).astype(F32)

    def units(s, carry):
        a = front_ref[s]
        for v in range(2):
            int_ref[UNIT + 2 * s + v] = 2 * jnp.maximum(a, 0) + v
        int_ref[FRONT + s] = a
        float_ref[HAS + s] = (a >= 0).astype(F32)
        return carry

    lax.fori_loop(0, 2 * SLOTS, units, 0)
    lane = lax.broadcasted_iota(jnp.int32, (192, NB), 1)

    def block(k, slot):
        a = slots[k * SLOTS + slot]
        off = pl.multiple_of(jnp.maximum(a, 0) * NB, NB)
        x = x_ref[k, :, pl.ds(off, NB)]
        return jnp.where(a >= 0, x, jnp.zeros_like(x))

    def panel(j, carry):
        x0 = block(0, j).astype(F32)
        x1 = block(1, j).astype(F32)
        r0 = pltpu.roll(x0, 64, 1)
        r1 = pltpu.roll(x1, 64, 1)
        pan_ref[2 * j] = jnp.where(lane < 64, x0, r1).astype(BF)
        pan_ref[2 * j + 1] = jnp.where(lane < 64, r0, x1).astype(BF)
        return carry

    lax.fori_loop(0, 8, panel, 0)

    def trail(m, carry):
        for k in range(2):
            for i in range(3):
                x = block(k, 8 + 3 * m + i)
                for s, t_ref in enumerate((t0_ref, t1_ref, t2_ref)):
                    t_ref[m, k, :, i * NB : (i + 1) * NB] = x[64 * s : 64 * s + 64]
        return carry

    lax.fori_loop(0, 16, trail, 0)


def pack(x, child_map, child_parent, pivot_order):
    t = jax.ShapeDtypeStruct((16, 2, 64, PC), BF)
    return pl.pallas_call(
        pack_kernel,
        out_shape=(
            jax.ShapeDtypeStruct((16, 192, NB), BF), t, t, t,
            jax.ShapeDtypeStruct((INTS,), jnp.int32), jax.ShapeDtypeStruct((FLOATS,), F32),
        ),
        in_specs=[vm(), sm(), sm(), sm()],
        out_specs=(vm(), vm(), vm(), vm(), sm(), sm()),
        scratch_shapes=[
            pltpu.SMEM((SLOTS,), jnp.int32),
            pltpu.SMEM((2 * SLOTS,), jnp.int32),
            pltpu.SMEM((KIDS // 2,), jnp.int32),
            pltpu.SMEM((KIDS,), jnp.int32),
            pltpu.SMEM((2 * SLOTS,), jnp.int32),
        ],
        compiler_params=pltpu.CompilerParams(vmem_limit_bytes=24 << 20),
        name="pack",
    )(x, child_map, child_parent, pivot_order)


def factor_block(m_ref, inv_ref, hook):
    rid = lax.broadcasted_iota(jnp.int32, (8, 1), 0)
    rows = [m_ref[8 * r : 8 * r + 8, :] for r in range(16)]
    for q in range(16):
        if q == 8:
            hook()
        c0 = 8 * q
        rb = [jnp.broadcast_to(rows[q][s : s + 1, :], (8, 2 * NB)) for s in range(8)]
        e = [
            [
                jnp.broadcast_to(rb[s][:, c0 + t : c0 + t + 1], (8, NB)) if t >= s else None
                for t in range(8)
            ]
            for s in range(8)
        ]
        inv = [None] * 8
        for t in range(8):
            inv[t] = 1.0 / e[t][t]
            for s in range(t + 1, 8):
                m = e[t][s] * inv[t]
                for u in range(s, 8):
                    e[s][u] = e[s][u] - m * e[t][u]
                rb[s] = rb[s] - jnp.concatenate([m, m], 1) * rb[t]
        new, iv = rb[7], inv[7]
        for s in range(6, -1, -1):
            new = jnp.where(rid == s, rb[s], new)
            iv = jnp.where(rid == s, inv[s], iv)
        m_ref[c0 : c0 + 8, :] = new
        inv_ref[c0 : c0 + 8, :] = iv
        if q < 15:
            cols = jnp.transpose(new[:, :NB] * iv)
            for r in range(q + 1, 16):
                p = [cols[8 * r : 8 * r + 8, t : t + 1] * rb[t] for t in range(8)]
                rows[r] = rows[r] - (
                    ((p[0] + p[1]) + (p[2] + p[3])) + ((p[4] + p[5]) + (p[6] + p[7]))
                )


class Gather:
    def __init__(self, own, out, send, recv, rows):
        self.own, self.out, self.send, self.recv, self.half = own, out, send, recv, rows // 2
        self.f = lax.axis_index("front")
        g = lax.axis_index("grid")
        self.x, self.y = g // 4, g % 4

    def dev(self, axis, d):
        if axis == 0:
            return (self.f, lax.rem(self.x + d, 4) * 4 + self.y)
        return (self.f, self.x * 4 + lax.rem(self.y + d, 4))

    def at(self, axis, d, r0, rn):
        x, y = self.x, self.y
        if axis == 0:
            x = lax.rem(x + d, 4)
        else:
            y = lax.rem(y + d, 4)
        return self.out.at[x, y, pl.ds(r0, rn), :]

    def line(self, axis, d, r0, rn):
        if axis == 0:
            return self.out.at[lax.rem(self.x + d, 4), :, pl.ds(r0, rn), :]
        return self.out.at[:, lax.rem(self.y + d, 4), pl.ds(r0, rn), :]

    def copy(self, src, dst, sem, axis, d):
        return pltpu.make_async_remote_copy(
            src_ref=src,
            dst_ref=dst,
            send_sem=self.send.at[sem],
            recv_sem=self.recv.at[sem],
            device_id=self.dev(axis, d),
            device_id_type=MESH,
        )

    def stage(self, n):
        h = self.half
        q = h // 2
        out = []
        for axis in range(2):
            r0 = axis * h
            other = 1 - axis
            b = axis * 8
            if n == 0:
                src = self.own.at[pl.ds(r0, h), :]
                for i, d in enumerate((1, 3, 2)):
                    out.append(self.copy(src, self.at(axis, 0, r0, h), b + i, axis, d))
            elif n == 1:
                a = self.line(other, 0, r0, h)
                out.append(self.copy(a, a, b + 3, other, 1))
                out.append(self.copy(a, a, b + 4, other, 3))
            else:
                a = self.line(other, 3, r0, q)
                out.append(self.copy(a, a, b + 5, other, 1))
                a = self.line(other, 1, r0 + q, q)
                out.append(self.copy(a, a, b + 6, other, 3))
        return out

    def start(self, n):
        for c in self.stage(n):
            c.start()

    def wait_recv(self, n):
        for c in self.stage(n):
            c.wait_recv()

    def wait_send(self):
        for n in range(3):
            for c in self.stage(n):
                c.wait_send()


class Swap:
    def __init__(self, axis, src, dst, send, recv, local):
        f, g = lax.axis_index("front"), lax.axis_index("grid")
        self.axis, self.f, self.g = axis, f, g
        self.me = g if axis == "grid" else f
        self.src, self.dst, self.send, self.recv, self.local = src, dst, send, recv, local

    def copy(self, i):
        if self.axis == "grid":
            to = lax.rem(self.g // 4 + i // 4, 4) * 4 + lax.rem(self.g % 4 + i % 4, 4)
            dev = (self.f, to)
        else:
            to = lax.rem(self.f // 2 + i // 2, 8) * 2 + lax.rem(self.f % 2 + i % 2, 2)
            dev = (to, self.g)
        return pltpu.make_async_remote_copy(
            src_ref=self.src.at[to],
            dst_ref=self.dst(self.me),
            send_sem=self.send.at[i],
            recv_sem=self.recv.at[i],
            device_id=dev,
            device_id_type=MESH,
        )

    def keep(self):
        return pltpu.make_async_copy(self.src.at[self.me], self.dst(self.me), self.local)

    def start(self):
        def one(i, c):
            self.copy(i).start()
            return c

        lax.fori_loop(1, 16, one, 0)
        self.keep().start()

    def wait_recv(self):
        def one(i, c):
            self.copy(i).wait_recv()
            return c

        lax.fori_loop(1, 16, one, 0)
        self.keep().wait()

    def wait_send(self):
        def one(i, c):
            self.copy(i).wait_send()
            return c

        lax.fori_loop(1, 16, one, 0)


def main_kernel(
    ps1, a0, a1, a2, od_ref, or_ref, ints, floats,
    ud_ref, ur_ref, s_ref, sg_ref, o0_ref, o1_ref, o2_ref,
    pr1, ps2, pr2, b0, b1, b2, c0, c1, c2, dsnd, psnd, prcv,
    w, m_ref, inv_ref, uh, ul, st, dall,
    asend, arecv, dsend, drecv, ssend, srecv, lsem, ksem,
):
    f = lax.axis_index("front")
    g = lax.axis_index("grid")
    x, y = g // 4, g % 4
    barrier = pltpu.get_barrier_semaphore()

    def greet(i, c):
        to = lax.rem(g + i, 16)
        pl.semaphore_signal(barrier, inc=1, device_id=(f, to), device_id_type=MESH)
        to = lax.rem(f + i, 16)
        pl.semaphore_signal(barrier, inc=1, device_id=(to, g), device_id_type=MESH)
        return c

    lax.fori_loop(1, 16, greet, 0)

    def swap(n, axis, src, dst):
        return Swap(axis, src, dst, asend.at[n], arecv.at[n], ksem.at[n])

    lane = lax.broadcasted_iota(jnp.int32, (192, NB), 1)

    panel1 = swap(0, "grid", ps1, lambda me: pr1.at[me])
    panel2 = swap(1, "front", ps2, lambda me: pr2.at[pl.ds(3 * me, 3)])
    pswap = swap(2, "grid", psnd, lambda me: prcv.at[pl.ds(64 * me, 64), :])

    def trail1(s):
        dst = (b0, b1, b2)[s]
        return swap(3 + s, "grid", (a0, a1, a2)[s], lambda me: dst.at[pl.ds(2 * me, 2)])

    def trail2(s):
        dst = (o0_ref, o1_ref, o2_ref)[s]
        return swap(6 + s, "front", (c0, c1, c2)[s], lambda me: dst.at[me])

    pl.semaphore_wait(barrier, 30)
    panel1.start()

    trail1(0).start()
    trail1(1).start()
    panel1.wait_recv()

    def sort_panel(p, carry):
        x0 = pr1[ints[SOURCE + 2 * p]].astype(F32)
        x1 = pr1[ints[SOURCE + 2 * p + 1]].astype(F32)
        m0 = floats[2 * p]
        m1 = floats[2 * p + 1]
        x0 = x0 * (1.0 - m0) + pltpu.roll(x0, 64, 1) * m0
        x1 = x1 * m1 + pltpu.roll(x1, 64, 1) * (1.0 - m1)
        z = jnp.where(lane < 64, x0, x1).astype(BF)
        for v in range(3):
            ps2[p, v] = z[64 * v : 64 * v + 64]
        return carry

    lax.fori_loop(0, 16, sort_panel, 0)
    panel2.start()

    def sort_trail(s):
        trail1(s).wait_recv()
        src, dst = (b0, b1, b2)[s], (c0, c1, c2)[s]

        def one(p, carry):
            for t in range(2):
                dst[p, t] = src[ints[ORDER + 2 * p + t]]
            return carry

        lax.fori_loop(0, 16, one, 0)
        trail2(s).start()

    sort_trail(0)
    panel2.wait_recv()

    def pivot_rows(slot):
        halves = []
        for v in range(2):
            total = jnp.zeros((64, NB), F32)
            for t in range(2):
                z = pr2[ints[UNIT + 2 * (t * SLOTS + slot) + v]].astype(F32)
                if t == 1:
                    z = pltpu.roll(z, 64, 1)
                total = total + z * floats[HAS + t * SLOTS + slot]
            halves.append(total)
        return jnp.transpose(jnp.concatenate(halves, 0))[:64]

    for i in range(5):
        j = lax.rem(g // 2 + i, 8)
        od = od_ref[:, pl.ds(pl.multiple_of(j * NB, NB), NB)].astype(F32)
        dsnd[:, i * NB : (i + 1) * NB] = pivot_rows(j) + od
    gd = Gather(dsnd, dall, dsend, drecv, 64)
    gd.start(0)
    dall[x, y] = dsnd[...]

    def rest(m, carry):
        for i in range(3):
            psnd[m, :, i * NB : (i + 1) * NB] = pivot_rows(8 + 3 * m + i)
        return carry

    lax.fori_loop(0, 16, rest, 0)
    for n in range(2):
        gd.wait_recv(n)
        gd.start(n + 1)
    pswap.start()
    trail1(2).start()
    sort_trail(1)
    gd.wait_recv(2)

    def cyclic(r, i):
        return jnp.concatenate(
            [dall[b // 4, b % 4, :, i * NB : (i + 1) * NB] for b in (2 * r, 2 * r + 1)], 0
        )

    for r in range(8):
        for c in range(8):
            if c < r:
                z = jnp.zeros((NB, NB), F32)
            elif c - r <= 4:
                z = cyclic(r, c - r)
            else:
                z = jnp.transpose(cyclic(c, 8 - (c - r)))
            w[r * NB : (r + 1) * NB, c * NB : (c + 1) * NB] = z
    eye = (
        lax.broadcasted_iota(jnp.int32, (NB, NB), 0) == lax.broadcasted_iota(jnp.int32, (NB, NB), 1)
    ).astype(F32)

    def gs(k):
        return Gather(st.at[k], sg_ref.at[k], ssend.at[k], srecv.at[k], PC)

    def local(k):
        return pltpu.make_async_copy(st.at[k], sg_ref.at[k, x, y], lsem.at[k])

    def move(k, n):
        c = gs(k)
        c.wait_recv(n - 1)
        if n == 1:
            local(k).wait()
        c.start(n)

    def step(k, carry):
        r0 = pl.multiple_of(k * NB, NB)
        m_ref[:, :NB] = w[pl.ds(r0, NB), pl.ds(r0, NB)]
        m_ref[:, NB:] = eye

        def hook():
            @pl.when(k >= 1)
            def _():
                move(k - 1, 1)

        factor_block(m_ref, inv_ref, hook)

        @pl.when(k == 0)
        def _():
            pswap.wait_recv()
            w[:, N:] = prcv[...] + or_ref[0].astype(F32)

        @pl.when(k == 2)
        def _():
            sort_trail(2)

        lh, ll = split(m_ref[:, NB:])
        ah, al = split(w[pl.ds(r0, NB), :])
        u = dg(lh, ah, 1, 0) + (dg(lh, al, 1, 0) + dg(ll, ah, 1, 0))
        w[pl.ds(r0, NB), :] = u
        h, l = split(u)
        uh[...] = h
        ul[...] = l
        iv = inv_ref[...]
        top = u[:, N:]
        ur_ref[pl.ds(r0, NB), :] = top
        rs = jnp.sqrt(iv)
        solved = top * jnp.concatenate([rs] * 3, 1)
        s_ref[pl.ds(r0, NB), :] = solved.astype(BF)
        st[k] = jnp.transpose(solved).astype(BF)
        gs(k).start(0)
        local(k).start()

        def upd(i, c):
            i0 = pl.multiple_of(i * NB, NB)
            xh, xl = split((uh[:, pl.ds(i0, NB)].astype(F32) + ul[:, pl.ds(i0, NB)].astype(F32)) * iv)
            d = dg(xh, uh[...], 0, 0) + (dg(xh, ul[...], 0, 0) + dg(xl, uh[...], 0, 0))
            w[pl.ds(i0, NB), :] = w[pl.ds(i0, NB), :] - d
            return c

        lax.fori_loop(k + 1, N // NB, upd, 0)

        @pl.when(k >= 1)
        def _():
            move(k - 1, 2)

        return carry

    last = N // NB - 1
    lax.fori_loop(0, N // NB, step, 0)
    move(last, 1)
    blk = pl.multiple_of((g // 2) * NB, NB)
    col = 64 * g + lax.broadcasted_iota(jnp.int32, (64, NB), 0)
    for r in range(8):
        own = jnp.transpose(w[r * NB : (r + 1) * NB, pl.ds(blk, NB)])
        own = jnp.where(g % 2 == 1, own[64:], own[:64])
        row = r * NB + lax.broadcasted_iota(jnp.int32, (64, NB), 1)
        ud_ref[:, r * NB : (r + 1) * NB] = jnp.where(row <= col, own, 0.0)
    move(last, 2)
    for s in range(3):
        trail1(s).wait_send()
        trail2(s).wait_send()
        trail2(s).wait_recv()
    for e in (panel1, panel2, pswap):
        e.wait_send()
    gd.wait_send()

    def finish(k, carry):
        c = gs(k)
        c.wait_recv(2)
        c.wait_send()
        return carry

    lax.fori_loop(0, N // NB, finish, 0)


def main_call(ps1, a0, a1, a2, orig_diag, orig_rows, *tables):
    steps = N // NB
    hbm = pl.BlockSpec(memory_space=pl.ANY)
    out = jax.ShapeDtypeStruct((16, 2, 64, PC), BF)
    panel = pltpu.VMEM((16, 192, NB), BF)
    send = pltpu.VMEM((16, 2, 64, PC), BF)
    recv = pltpu.VMEM((KIDS, 64, PC), BF)
    sems = pltpu.SemaphoreType.DMA
    return pl.pallas_call(
        main_kernel,
        out_shape=(
            jax.ShapeDtypeStruct((64, N), F32),
            jax.ShapeDtypeStruct((N, PC), F32),
            jax.ShapeDtypeStruct((N, PC), BF),
            jax.ShapeDtypeStruct((steps, 4, 4, PC, NB), BF),
            out, out, out,
        ),
        in_specs=[vm(), vm(), vm(), vm(), vm(), vm(), sm(), sm()],
        out_specs=(vm(), vm(), vm(), hbm, vm(), vm(), vm()),
        scratch_shapes=[
            panel, pltpu.VMEM((16, 3, 64, NB), BF), pltpu.VMEM((48, 64, NB), BF),
            recv, recv, recv, send, send, send,
            pltpu.VMEM((64, PW), F32),
            pltpu.VMEM((16, 64, PC), F32),
            pltpu.VMEM((N, PC), F32),
            pltpu.VMEM((N, WT), F32),
            pltpu.VMEM((NB, 2 * NB), F32),
            pltpu.VMEM((NB, NB), F32),
            pltpu.VMEM((NB, WT), BF),
            pltpu.VMEM((NB, WT), BF),
            pltpu.VMEM((steps, PC, NB), BF),
            pltpu.VMEM((4, 4, 64, PW), F32),
            sems((9, 16)), sems((9, 16)), sems((16,)), sems((16,)),
            sems((steps, 16)), sems((steps, 16)), sems((steps,)), sems((9,)),
        ],
        compiler_params=pltpu.CompilerParams(
            vmem_limit_bytes=40 << 20, collective_id=0, has_side_effects=True
        ),
        name="assemble_factor_gather",
    )(ps1, a0, a1, a2, orig_diag, orig_rows, *tables)


def schur_kernel(
    sg_ref, s_ref, t0_ref, t1_ref, t2_ref, ud_ref, ur_ref, slots, o_ref, udo_ref, uro_ref
):
    m = pl.program_id(0)
    uro_ref[0] = ur_ref[...]
    udo_ref[...] = ud_ref[...]
    lhs = jnp.concatenate([sg_ref[k, 0] for k in range(N // NB)], 1)
    prod = dg(lhs, s_ref[...], 1, 0)
    for i in range(3):
        for v in range(2):
            total = -prod[i * NB + v * 64 : i * NB + v * 64 + 64]
            for t in range(2):
                a = slots[FRONT + t * SLOTS + 8 + 3 * m + i]
                u = 2 * jnp.maximum(a, 0) + v
                s = u % 3
                x = jnp.where(
                    s == 0, t0_ref[u // 3, t], jnp.where(s == 1, t1_ref[u // 3, t], t2_ref[u // 3, t])
                )
                total = total + jnp.where(a >= 0, x.astype(F32), 0.0)
            o_ref[0, i * NB + v * 64 : i * NB + v * 64 + 64, :] = total.astype(BF)


def schur_call(sg, s, t0, t1, t2, ud, ur, ints):
    steps = N // NB
    return pl.pallas_call(
        schur_kernel,
        out_shape=(
            jax.ShapeDtypeStruct((1, 16 * PC, PC), BF),
            jax.ShapeDtypeStruct((64, N), F32),
            jax.ShapeDtypeStruct((1, N, PC), F32),
        ),
        grid=(16,),
        in_specs=[
            pl.BlockSpec((steps, 1, PC, NB), lambda m: (0, m, 0, 0)),
            vm(), vm(), vm(), vm(),
            pl.BlockSpec((64, NB), lambda m: (0, m // 2)),
            pl.BlockSpec((64, PC), lambda m: (m, 0)),
            sm(),
        ],
        out_specs=(
            pl.BlockSpec((1, PC, PC), lambda m: (0, m, 0)),
            pl.BlockSpec((64, NB), lambda m: (0, m // 2)),
            pl.BlockSpec((1, 64, PC), lambda m: (0, m, 0)),
        ),
        compiler_params=pltpu.CompilerParams(vmem_limit_bytes=46 << 20),
        name="schur",
    )(sg.reshape(steps, 16, PC, NB), s, t0, t1, t2, ud, ur, ints)


def shards(child_blocks, orig_diag, orig_rows, child_map, child_parent, pivot_order):
    panel, a0, a1, a2, ints, floats = pack(child_blocks, child_map, child_parent, pivot_order)
    upper_diag, upper_rows, s, sg, *trail = main_call(
        panel, a0, a1, a2, orig_diag[0].T, orig_rows, ints, floats
    )
    schur, upper_diag, upper_rows = schur_call(sg, s, *trail, upper_diag, upper_rows, ints)
    return upper_diag.T[None], upper_rows, schur


def solution(mesh):
    return jax.shard_map(
        shards,
        mesh=mesh,
        in_specs=(
            P("grid", "front", None),
            P("front", None, "grid"),
            P("front", None, "grid"),
            P(),
            P(),
            P(),
        ),
        out_specs=(P("front", None, "grid"), P("front", None, "grid"), P("front", None, "grid")),
        check_vma=False,
    )
```

```python
import functools

import jax
import jax.numpy as jnp
from jax import lax
from jax.experimental import pallas as pl
from jax.experimental.pallas import tpu as pltpu
from jax.sharding import PartitionSpec as P

N = 1024
NB = 128
PC = 384
WT = N + PC
SLOTS = 56
KB = 24
KIDS = 32
ORDER = 0
SOURCE = ORDER + KIDS
UNIT = SOURCE + KIDS
FRONT = UNIT + 4 * SLOTS
INTS = FRONT + 2 * SLOTS
HAS = KIDS
FLOATS = HAS + 2 * SLOTS
PW = 5 * NB
F32 = jnp.float32
BF = jnp.bfloat16
MESH = pl.DeviceIdType.MESH


def vm():
    return pl.BlockSpec(memory_space=pltpu.VMEM)


def sm():
    return pl.BlockSpec(memory_space=pltpu.SMEM)


def split(x):
    hi = x.astype(BF)
    return hi, (x - hi.astype(F32)).astype(BF)


def dg(a, b, ca, cb):
    return lax.dot_general(a, b, (((ca,), (cb,)), ((), ())), preferred_element_type=F32)


def kid_order_table(parent_ref, order, count):
    for p in range(KIDS // 2):
        count[p] = 0
    for c in range(KIDS):
        p = parent_ref[c]
        n = count[p]
        order[2 * p + n] = c
        count[p] = n + 1


def slot_table(child, parent, map_ref, piv_ref, tab, slots, base):
    for v in range(SLOTS):
        tab[v] = -1
    for a in range(KB):
        tab[map_ref[child, a]] = a
    for s in range(SLOTS):
        slots[base + s] = tab[piv_ref[parent, s]]


def own_slots(parent_ref, map_ref, piv_ref, tab, slots, order, count):
    f = lax.axis_index("front")
    kid_order_table(parent_ref, order, count)
    for t in range(2):
        slot_table(order[2 * f + t], f, map_ref, piv_ref, tab, slots, t * SLOTS)


def pack_kernel(
    x_ref, map_ref, parent_ref, piv_ref,
    pan_ref, t0_ref, t1_ref, t2_ref, int_ref, float_ref,
    tab, slots, count, order_ref, front_ref,
):
    g = lax.axis_index("grid")
    for k in range(2):
        c = 2 * g + k
        slot_table(c, parent_ref[c], map_ref, piv_ref, tab, slots, k * SLOTS)
    own_slots(parent_ref, map_ref, piv_ref, tab, front_ref, order_ref, count)
    for c in range(KIDS):
        int_ref[ORDER + c] = order_ref[c]
        int_ref[SOURCE + c] = order_ref[c] // 2
        float_ref[c] = (order_ref[c] % 2).astype(F32)

    def units(s, carry):
        a = front_ref[s]
        for v in range(2):
            int_ref[UNIT + 2 * s + v] = 2 * jnp.maximum(a, 0) + v
        int_ref[FRONT + s] = a
        float_ref[HAS + s] = (a >= 0).astype(F32)
        return carry

    lax.fori_loop(0, 2 * SLOTS, units, 0)
    lane = lax.broadcasted_iota(jnp.int32, (192, NB), 1)

    def block(k, slot):
        a = slots[k * SLOTS + slot]
        off = pl.multiple_of(jnp.maximum(a, 0) * NB, NB)
        x = x_ref[k, :, pl.ds(off, NB)]
        return jnp.where(a >= 0, x, jnp.zeros_like(x))

    def panel(j, carry):
        x0 = block(0, j).astype(F32)
        x1 = block(1, j).astype(F32)
        r0 = pltpu.roll(x0, 64, 1)
        r1 = pltpu.roll(x1, 64, 1)
        pan_ref[2 * j] = jnp.where(lane < 64, x0, r1).astype(BF)
        pan_ref[2 * j + 1] = jnp.where(lane < 64, r0, x1).astype(BF)
        return carry

    lax.fori_loop(0, 8, panel, 0)

    def trail(m, carry):
        for k in range(2):
            for i in range(3):
                x = block(k, 8 + 3 * m + i)
                for s, t_ref in enumerate((t0_ref, t1_ref, t2_ref)):
                    t_ref[m, k, :, i * NB : (i + 1) * NB] = x[64 * s : 64 * s + 64]
        return carry

    lax.fori_loop(0, 16, trail, 0)


def pack(x, child_map, child_parent, pivot_order):
    t = jax.ShapeDtypeStruct((16, 2, 64, PC), BF)
    return pl.pallas_call(
        pack_kernel,
        out_shape=(
            jax.ShapeDtypeStruct((16, 192, NB), BF), t, t, t,
            jax.ShapeDtypeStruct((INTS,), jnp.int32), jax.ShapeDtypeStruct((FLOATS,), F32),
        ),
        in_specs=[vm(), sm(), sm(), sm()],
        out_specs=(vm(), vm(), vm(), vm(), sm(), sm()),
        scratch_shapes=[
            pltpu.SMEM((SLOTS,), jnp.int32),
            pltpu.SMEM((2 * SLOTS,), jnp.int32),
            pltpu.SMEM((KIDS // 2,), jnp.int32),
            pltpu.SMEM((KIDS,), jnp.int32),
            pltpu.SMEM((2 * SLOTS,), jnp.int32),
        ],
        compiler_params=pltpu.CompilerParams(vmem_limit_bytes=24 << 20),
        name="pack",
    )(x, child_map, child_parent, pivot_order)


def factor_block(m_ref, inv_ref, hook):
    rid = lax.broadcasted_iota(jnp.int32, (8, 1), 0)
    rows = [m_ref[8 * r : 8 * r + 8, :] for r in range(16)]
    for q in range(16):
        if q == 8:
            hook()
        c0 = 8 * q
        rb = [jnp.broadcast_to(rows[q][s : s + 1, :], (8, 2 * NB)) for s in range(8)]
        e = [
            [
                jnp.broadcast_to(rb[s][:, c0 + t : c0 + t + 1], (8, NB)) if t >= s else None
                for t in range(8)
            ]
            for s in range(8)
        ]
        inv = [None] * 8
        for t in range(8):
            inv[t] = 1.0 / e[t][t]
            for s in range(t + 1, 8):
                m = e[t][s] * inv[t]
                for u in range(s, 8):
                    e[s][u] = e[s][u] - m * e[t][u]
                rb[s] = rb[s] - jnp.concatenate([m, m], 1) * rb[t]
        new, iv = rb[7], inv[7]
        for s in range(6, -1, -1):
            new = jnp.where(rid == s, rb[s], new)
            iv = jnp.where(rid == s, inv[s], iv)
        m_ref[c0 : c0 + 8, :] = new
        inv_ref[c0 : c0 + 8, :] = iv
        if q < 15:
            cols = jnp.transpose(new[:, :NB] * iv)
            for r in range(q + 1, 16):
                p = [cols[8 * r : 8 * r + 8, t : t + 1] * rb[t] for t in range(8)]
                rows[r] = rows[r] - (
                    ((p[0] + p[1]) + (p[2] + p[3])) + ((p[4] + p[5]) + (p[6] + p[7]))
                )


class Gather:
    def __init__(self, own, out, send, recv, rows):
        self.own, self.out, self.send, self.recv, self.half = own, out, send, recv, rows // 2
        self.f = lax.axis_index("front")
        g = lax.axis_index("grid")
        self.x, self.y = g // 4, g % 4

    def dev(self, axis, d):
        if axis == 0:
            return (self.f, lax.rem(self.x + d, 4) * 4 + self.y)
        return (self.f, self.x * 4 + lax.rem(self.y + d, 4))

    def at(self, axis, d, r0, rn):
        x, y = self.x, self.y
        if axis == 0:
            x = lax.rem(x + d, 4)
        else:
            y = lax.rem(y + d, 4)
        return self.out.at[x, y, pl.ds(r0, rn), :]

    def line(self, axis, d, r0, rn):
        if axis == 0:
            return self.out.at[lax.rem(self.x + d, 4), :, pl.ds(r0, rn), :]
        return self.out.at[:, lax.rem(self.y + d, 4), pl.ds(r0, rn), :]

    def copy(self, src, dst, sem, axis, d):
        return pltpu.make_async_remote_copy(
            src_ref=src,
            dst_ref=dst,
            send_sem=self.send.at[sem],
            recv_sem=self.recv.at[sem],
            device_id=self.dev(axis, d),
            device_id_type=MESH,
        )

    def stage(self, n):
        h = self.half
        q = h // 2
        out = []
        for axis in range(2):
            r0 = axis * h
            other = 1 - axis
            b = axis * 8
            if n == 0:
                src = self.own.at[pl.ds(r0, h), :]
                for i, d in enumerate((1, 3, 2)):
                    out.append(self.copy(src, self.at(axis, 0, r0, h), b + i, axis, d))
            elif n == 1:
                a = self.line(other, 0, r0, h)
                out.append(self.copy(a, a, b + 3, other, 1))
                out.append(self.copy(a, a, b + 4, other, 3))
            else:
                a = self.line(other, 3, r0, q)
                out.append(self.copy(a, a, b + 5, other, 1))
                a = self.line(other, 1, r0 + q, q)
                out.append(self.copy(a, a, b + 6, other, 3))
        return out

    def start(self, n):
        for c in self.stage(n):
            c.start()

    def wait_recv(self, n):
        for c in self.stage(n):
            c.wait_recv()

    def wait_send(self):
        for n in range(3):
            for c in self.stage(n):
                c.wait_send()


class Swap:
    def __init__(self, axis, src, dst, send, recv, local):
        f, g = lax.axis_index("front"), lax.axis_index("grid")
        self.axis, self.f, self.g = axis, f, g
        self.me = g if axis == "grid" else f
        self.src, self.dst, self.send, self.recv, self.local = src, dst, send, recv, local

    def copy(self, i):
        if self.axis == "grid":
            to = lax.rem(self.g // 4 + i // 4, 4) * 4 + lax.rem(self.g % 4 + i % 4, 4)
            dev = (self.f, to)
        else:
            to = lax.rem(self.f // 2 + i // 2, 8) * 2 + lax.rem(self.f % 2 + i % 2, 2)
            dev = (to, self.g)
        return pltpu.make_async_remote_copy(
            src_ref=self.src.at[to],
            dst_ref=self.dst(self.me),
            send_sem=self.send.at[i],
            recv_sem=self.recv.at[i],
            device_id=dev,
            device_id_type=MESH,
        )

    def keep(self):
        return pltpu.make_async_copy(self.src.at[self.me], self.dst(self.me), self.local)

    def start(self):
        def one(i, c):
            self.copy(i).start()
            return c

        lax.fori_loop(1, 16, one, 0)
        self.keep().start()

    def wait_recv(self):
        def one(i, c):
            self.copy(i).wait_recv()
            return c

        lax.fori_loop(1, 16, one, 0)
        self.keep().wait()

    def wait_send(self):
        def one(i, c):
            self.copy(i).wait_send()
            return c

        lax.fori_loop(1, 16, one, 0)


def main_kernel(
    ps1, a0, a1, a2, od_ref, or_ref, ints, floats,
    ud_ref, ur_ref, s_ref, sg_ref, acc_ref, end_ref,
    pr1, ps2, pr2, b0, b1, b2, c0, c1, c2, dsnd, psnd,
    w, m_ref, inv_ref, uh, ul, st, dall, tin, sv,
    asend, arecv, dsend, drecv, ssend, srecv, lsem, ksem, vsem,
):
    f = lax.axis_index("front")
    g = lax.axis_index("grid")
    x, y = g // 4, g % 4
    barrier = pltpu.get_barrier_semaphore()

    def greet(i, c):
        to = lax.rem(g + i, 16)
        pl.semaphore_signal(barrier, inc=1, device_id=(f, to), device_id_type=MESH)
        to = lax.rem(f + i, 16)
        pl.semaphore_signal(barrier, inc=1, device_id=(to, g), device_id_type=MESH)
        return c

    lax.fori_loop(1, 16, greet, 0)

    def swap(n, axis, src, dst):
        return Swap(axis, src, dst, asend.at[n], arecv.at[n], ksem.at[n])

    lane = lax.broadcasted_iota(jnp.int32, (192, NB), 1)

    panel1 = swap(0, "grid", ps1, lambda me: pr1.at[me])
    panel2 = swap(1, "front", ps2, lambda me: pr2.at[pl.ds(3 * me, 3)])
    pswap = swap(2, "grid", psnd, lambda me: w.at[pl.ds(64 * me, 64), pl.ds(N, PC)])

    def trail1(s):
        dst = (b0, b1, b2)[s]
        return swap(3 + s, "grid", (a0, a1, a2)[s], lambda me: dst.at[pl.ds(2 * me, 2)])

    def trail2(s):
        return swap(6 + s, "front", (c0, c1, c2)[s], lambda me: tin.at[3 * me + s])

    pl.semaphore_wait(barrier, 30)
    panel1.start()

    trail1(0).start()
    trail1(1).start()
    panel1.wait_recv()

    def sort_panel(p, carry):
        x0 = pr1[ints[SOURCE + 2 * p]].astype(F32)
        x1 = pr1[ints[SOURCE + 2 * p + 1]].astype(F32)
        m0 = floats[2 * p]
        m1 = floats[2 * p + 1]
        x0 = x0 * (1.0 - m0) + pltpu.roll(x0, 64, 1) * m0
        x1 = x1 * m1 + pltpu.roll(x1, 64, 1) * (1.0 - m1)
        z = jnp.where(lane < 64, x0, x1).astype(BF)
        for v in range(3):
            ps2[p, v] = z[64 * v : 64 * v + 64]
        return carry

    lax.fori_loop(0, 16, sort_panel, 0)
    panel2.start()

    def sort_trail(s):
        trail1(s).wait_recv()
        src, dst = (b0, b1, b2)[s], (c0, c1, c2)[s]

        def one(p, carry):
            for t in range(2):
                dst[p, t] = src[ints[ORDER + 2 * p + t]]
            return carry

        lax.fori_loop(0, 16, one, 0)
        trail2(s).start()

    sort_trail(0)
    panel2.wait_recv()

    def pivot_rows(slot):
        halves = []
        for v in range(2):
            total = jnp.zeros((64, NB), F32)
            for t in range(2):
                z = pr2[ints[UNIT + 2 * (t * SLOTS + slot) + v]].astype(F32)
                if t == 1:
                    z = pltpu.roll(z, 64, 1)
                total = total + z * floats[HAS + t * SLOTS + slot]
            halves.append(total)
        return jnp.transpose(jnp.concatenate(halves, 0))[:64]

    for i in range(5):
        j = lax.rem(g // 2 + i, 8)
        od = od_ref[:, pl.ds(pl.multiple_of(j * NB, NB), NB)].astype(F32)
        dsnd[:, i * NB : (i + 1) * NB] = pivot_rows(j) + od
    gd = Gather(dsnd, dall, dsend, drecv, 64)
    gd.start(0)
    dall[x, y] = dsnd[...]

    def rest(m, carry):
        for i in range(3):
            psnd[m, :, i * NB : (i + 1) * NB] = pivot_rows(8 + 3 * m + i)
        return carry

    lax.fori_loop(0, 16, rest, 0)
    for n in range(2):
        gd.wait_recv(n)
        gd.start(n + 1)
    pswap.start()
    trail1(2).start()
    sort_trail(1)
    gd.wait_recv(2)

    def cyclic(r, i):
        return jnp.concatenate(
            [dall[b // 4, b % 4, :, i * NB : (i + 1) * NB] for b in (2 * r, 2 * r + 1)], 0
        )

    for r in range(8):
        for c in range(8):
            if c < r:
                z = jnp.zeros((NB, NB), F32)
            elif c - r <= 4:
                z = cyclic(r, c - r)
            else:
                z = jnp.transpose(cyclic(c, 8 - (c - r)))
            w[r * NB : (r + 1) * NB, c * NB : (c + 1) * NB] = z
    eye = (
        lax.broadcasted_iota(jnp.int32, (NB, NB), 0) == lax.broadcasted_iota(jnp.int32, (NB, NB), 1)
    ).astype(F32)

    def gs(k):
        return Gather(st.at[k], sg_ref.at[k], ssend.at[k], srecv.at[k], PC)

    def local(k):
        return pltpu.make_async_copy(st.at[k], sg_ref.at[k, x, y], lsem.at[k])

    def move(k, n):
        c = gs(k)
        c.wait_recv(n - 1)
        if n == 1:
            local(k).wait()
        c.start(n)

    def load(n):
        return pltpu.make_async_copy(sg_ref.at[pl.ds(2 * n, 2)], (sv, end_ref)[n % 2], vsem.at[n % 2])

    def fetch(n):
        for k in (2 * n, 2 * n + 1):
            gs(k).wait_recv(2)
        load(n).start()

    def product(n, m):
        lhs = jnp.concatenate([(sv, end_ref)[n % 2][k, m // 4, m % 4] for k in range(2)], 1)
        return dg(lhs, s_ref[2 * NB * n : 2 * NB * (n + 1), :], 1, 0)

    def step(k, carry):
        r0 = pl.multiple_of(k * NB, NB)
        m_ref[:, :NB] = w[pl.ds(r0, NB), pl.ds(r0, NB)]
        m_ref[:, NB:] = eye

        def hook():
            @pl.when(k >= 1)
            def _():
                move(k - 1, 1)

        factor_block(m_ref, inv_ref, hook)

        @pl.when(k == N // NB - 1)
        def _():
            fetch(0)
            fetch(1)

        @pl.when(k == 0)
        def _():
            pswap.wait_recv()
            w[:, N:] = w[:, N:] + or_ref[0].astype(F32)

        @pl.when(k == 2)
        def _():
            sort_trail(2)

        lh, ll = split(m_ref[:, NB:])
        ah, al = split(w[pl.ds(r0, NB), :])
        u = dg(lh, ah, 1, 0) + (dg(lh, al, 1, 0) + dg(ll, ah, 1, 0))
        w[pl.ds(r0, NB), :] = u
        h, l = split(u)
        uh[...] = h
        ul[...] = l
        iv = inv_ref[...]
        top = u[:, N:]
        ur_ref[pl.ds(r0, NB), :] = top
        rs = jnp.sqrt(iv)
        solved = top * jnp.concatenate([rs] * 3, 1)
        s_ref[pl.ds(r0, NB), :] = solved.astype(BF)
        st[k] = jnp.transpose(solved).astype(BF)
        gs(k).start(0)
        local(k).start()

        def upd(i, c):
            i0 = pl.multiple_of(i * NB, NB)
            xh, xl = split((uh[:, pl.ds(i0, NB)].astype(F32) + ul[:, pl.ds(i0, NB)].astype(F32)) * iv)
            d = dg(xh, uh[...], 0, 0) + (dg(xh, ul[...], 0, 0) + dg(xl, uh[...], 0, 0))
            w[pl.ds(i0, NB), :] = w[pl.ds(i0, NB), :] - d
            return c

        lax.fori_loop(k + 1, N // NB, upd, 0)

        @pl.when(k >= 1)
        def _():
            move(k - 1, 2)

        return carry

    last = N // NB - 1
    lax.fori_loop(0, N // NB, step, 0)
    load(0).wait()

    def first(m, c):
        acc_ref[pl.ds(pl.multiple_of(m * PC, PC), PC), :] = product(0, m)
        return c

    lax.fori_loop(0, 16, first, 0)
    fetch(2)
    move(last, 1)
    load(1).wait()

    def second(m, c):
        rows = pl.ds(pl.multiple_of(m * PC, PC), PC)
        acc_ref[rows, :] = acc_ref[rows, :] + product(1, m)
        return c

    lax.fori_loop(0, 16, second, 0)
    move(last, 2)
    blk = pl.multiple_of((g // 2) * NB, NB)
    col = 64 * g + lax.broadcasted_iota(jnp.int32, (64, NB), 0)
    for r in range(8):
        own = jnp.transpose(w[r * NB : (r + 1) * NB, pl.ds(blk, NB)])
        own = jnp.where(g % 2 == 1, own[64:], own[:64])
        row = r * NB + lax.broadcasted_iota(jnp.int32, (64, NB), 1)
        ud_ref[:, r * NB : (r + 1) * NB] = jnp.where(row <= col, own, 0.0)
    for s in range(3):
        trail1(s).wait_send()
        trail2(s).wait_send()
        trail2(s).wait_recv()
    load(2).wait()

    def third(m, c):
        for i in range(3):
            for v in range(2):
                r = i * NB + v * 64
                total = jnp.zeros((64, PC), F32)
                for t in range(2):
                    e = t * SLOTS + 8 + 3 * m + i
                    total = total + tin[ints[UNIT + 2 * e + v], t].astype(F32) * floats[HAS + e]
                rows = pl.ds(pl.multiple_of(m * PC + r, 64), 64)
                acc_ref[rows, :] = total - acc_ref[rows, :]
        rows = pl.ds(pl.multiple_of(m * PC, PC), PC)
        acc_ref[rows, :] = acc_ref[rows, :] - product(2, m)
        return c

    lax.fori_loop(0, 16, third, 0)
    for e in (panel1, panel2, pswap):
        e.wait_send()
    gd.wait_send()

    fetch(3)

    def finish(k, carry):
        gs(k).wait_send()
        return carry

    lax.fori_loop(0, N // NB, finish, 0)
    load(3).wait()


def main_call(ps1, a0, a1, a2, orig_diag, orig_rows, *tables):
    steps = N // NB
    hbm = pl.BlockSpec(memory_space=pl.ANY)
    panel = pltpu.VMEM((16, 192, NB), BF)
    send = pltpu.VMEM((16, 2, 64, PC), BF)
    recv = pltpu.VMEM((KIDS, 64, PC), BF)
    sems = pltpu.SemaphoreType.DMA
    return pl.pallas_call(
        main_kernel,
        out_shape=(
            jax.ShapeDtypeStruct((64, N), F32),
            jax.ShapeDtypeStruct((N, PC), F32),
            jax.ShapeDtypeStruct((N, PC), BF),
            jax.ShapeDtypeStruct((steps, 4, 4, PC, NB), BF),
            jax.ShapeDtypeStruct((16 * PC, PC), F32),
            jax.ShapeDtypeStruct((2, 4, 4, PC, NB), BF),
        ),
        in_specs=[vm(), vm(), vm(), vm(), vm(), vm(), sm(), sm()],
        out_specs=(vm(), vm(), vm(), hbm, vm(), vm()),
        scratch_shapes=[
            panel, pltpu.VMEM((16, 3, 64, NB), BF), pltpu.VMEM((48, 64, NB), BF),
            recv, recv, recv, send, send, send,
            pltpu.VMEM((64, PW), F32),
            pltpu.VMEM((16, 64, PC), F32),
            pltpu.VMEM((N, WT), F32),
            pltpu.VMEM((NB, 2 * NB), F32),
            pltpu.VMEM((NB, NB), F32),
            pltpu.VMEM((NB, WT), BF),
            pltpu.VMEM((NB, WT), BF),
            pltpu.VMEM((steps, PC, NB), BF),
            pltpu.VMEM((4, 4, 64, PW), F32),
            pltpu.VMEM((48, 2, 64, PC), BF),
            pltpu.VMEM((2, 4, 4, PC, NB), BF),
            sems((9, 16)), sems((9, 16)), sems((16,)), sems((16,)),
            sems((steps, 16)), sems((steps, 16)), sems((steps,)), sems((9,)), sems((2,)),
        ],
        compiler_params=pltpu.CompilerParams(
            vmem_limit_bytes=65 << 19, collective_id=0, has_side_effects=True
        ),
        name="assemble_factor_gather",
    )(ps1, a0, a1, a2, orig_diag, orig_rows, *tables)


def schur_kernel(end_ref, s_ref, acc_ref, ud_ref, ur_ref, o_ref, udo_ref, uro_ref):
    uro_ref[0] = ur_ref[...]
    udo_ref[...] = ud_ref[...]
    m = pl.program_id(0)
    for i in range(2):
        b = 2 * m + i
        lhs = jnp.concatenate([end_ref[k, b] for k in range(2)], 1)
        rows = pl.ds(pl.multiple_of(b * PC, PC), PC)
        o_ref[0, i * PC : (i + 1) * PC, :] = (
            acc_ref[rows, :] - dg(lhs, s_ref[6 * NB :, :], 1, 0)
        ).astype(BF)


def schur_call(end, s, acc, ud, ur):
    return pl.pallas_call(
        schur_kernel,
        out_shape=(
            jax.ShapeDtypeStruct((1, 16 * PC, PC), BF),
            jax.ShapeDtypeStruct((64, N), F32),
            jax.ShapeDtypeStruct((1, N, PC), F32),
        ),
        grid=(8,),
        in_specs=[
            vm(),
            vm(),
            vm(),
            pl.BlockSpec((64, NB), lambda m: (0, m)),
            pl.BlockSpec((NB, PC), lambda m: (m, 0)),
        ],
        out_specs=(
            pl.BlockSpec((1, 2 * PC, PC), lambda m: (0, m, 0)),
            pl.BlockSpec((64, NB), lambda m: (0, m)),
            pl.BlockSpec((1, NB, PC), lambda m: (0, m, 0)),
        ),
        compiler_params=pltpu.CompilerParams(vmem_limit_bytes=20 << 20),
        name="schur",
    )(end.reshape(2, 16, PC, NB), s, acc, ud, ur)


def shards(child_blocks, orig_diag, orig_rows, child_map, child_parent, pivot_order):
    panel, a0, a1, a2, ints, floats = pack(child_blocks, child_map, child_parent, pivot_order)
    upper_diag, upper_rows, s, _, acc, end = main_call(
        panel, a0, a1, a2, orig_diag[0].T, orig_rows, ints, floats
    )
    schur, upper_diag, upper_rows = schur_call(end, s, acc, upper_diag, upper_rows)
    return upper_diag.T[None], upper_rows, schur


def solution(mesh):
    return jax.shard_map(
        shards,
        mesh=mesh,
        in_specs=(
            P("grid", "front", None),
            P("front", None, "grid"),
            P("front", None, "grid"),
            P(),
            P(),
            P(),
        ),
        out_specs=(P("front", None, "grid"), P("front", None, "grid"), P("front", None, "grid")),
        check_vma=False,
    )
```

```python
import functools

import jax
import jax.numpy as jnp
from jax import lax
from jax.experimental import pallas as pl
from jax.experimental.pallas import tpu as pltpu
from jax.sharding import PartitionSpec as P

N = 1024
NB = 128
PC = 384
WT = N + PC
SLOTS = 56
KB = 24
KIDS = 32
ORDER = 0
SOURCE = ORDER + KIDS
UNIT = SOURCE + KIDS
FRONT = UNIT + 4 * SLOTS
INTS = FRONT + 2 * SLOTS
HAS = KIDS
FLOATS = HAS + 2 * SLOTS
PW = 5 * NB
F32 = jnp.float32
BF = jnp.bfloat16
MESH = pl.DeviceIdType.MESH


def vm():
    return pl.BlockSpec(memory_space=pltpu.VMEM)


def sm():
    return pl.BlockSpec(memory_space=pltpu.SMEM)


def split(x):
    hi = x.astype(BF)
    return hi, (x - hi.astype(F32)).astype(BF)


def dg(a, b, ca, cb):
    return lax.dot_general(a, b, (((ca,), (cb,)), ((), ())), preferred_element_type=F32)


def kid_order_table(parent_ref, order, count):
    for p in range(KIDS // 2):
        count[p] = 0
    for c in range(KIDS):
        p = parent_ref[c]
        n = count[p]
        order[2 * p + n] = c
        count[p] = n + 1


def slot_table(child, parent, map_ref, piv_ref, tab, slots, base):
    for v in range(SLOTS):
        tab[v] = -1
    for a in range(KB):
        tab[map_ref[child, a]] = a
    for s in range(SLOTS):
        slots[base + s] = tab[piv_ref[parent, s]]


def own_slots(parent_ref, map_ref, piv_ref, tab, slots, order, count):
    f = lax.axis_index("front")
    kid_order_table(parent_ref, order, count)
    for t in range(2):
        slot_table(order[2 * f + t], f, map_ref, piv_ref, tab, slots, t * SLOTS)


def pack_kernel(
    x_ref, map_ref, parent_ref, piv_ref,
    pan_ref, t0_ref, t1_ref, t2_ref, int_ref, float_ref,
    tab, slots, count, order_ref, front_ref,
):
    g = lax.axis_index("grid")
    for k in range(2):
        c = 2 * g + k
        slot_table(c, parent_ref[c], map_ref, piv_ref, tab, slots, k * SLOTS)
    own_slots(parent_ref, map_ref, piv_ref, tab, front_ref, order_ref, count)
    for c in range(KIDS):
        int_ref[ORDER + c] = order_ref[c]
        int_ref[SOURCE + c] = order_ref[c] // 2
        float_ref[c] = (order_ref[c] % 2).astype(F32)

    def units(s, carry):
        a = front_ref[s]
        for v in range(2):
            int_ref[UNIT + 2 * s + v] = 2 * jnp.maximum(a, 0) + v
        int_ref[FRONT + s] = a
        float_ref[HAS + s] = (a >= 0).astype(F32)
        return carry

    lax.fori_loop(0, 2 * SLOTS, units, 0)
    lane = lax.broadcasted_iota(jnp.int32, (192, NB), 1)

    def block(k, slot):
        a = slots[k * SLOTS + slot]
        off = pl.multiple_of(jnp.maximum(a, 0) * NB, NB)
        x = x_ref[k, :, pl.ds(off, NB)]
        return jnp.where(a >= 0, x, jnp.zeros_like(x))

    def panel(j, carry):
        x0 = block(0, j).astype(F32)
        x1 = block(1, j).astype(F32)
        r0 = pltpu.roll(x0, 64, 1)
        r1 = pltpu.roll(x1, 64, 1)
        pan_ref[2 * j] = jnp.where(lane < 64, x0, r1).astype(BF)
        pan_ref[2 * j + 1] = jnp.where(lane < 64, r0, x1).astype(BF)
        return carry

    lax.fori_loop(0, 8, panel, 0)

    def trail(m, carry):
        for k in range(2):
            for i in range(3):
                x = block(k, 8 + 3 * m + i)
                for s, t_ref in enumerate((t0_ref, t1_ref, t2_ref)):
                    t_ref[m, k, :, i * NB : (i + 1) * NB] = x[64 * s : 64 * s + 64]
        return carry

    lax.fori_loop(0, 16, trail, 0)


def pack(x, child_map, child_parent, pivot_order):
    t = jax.ShapeDtypeStruct((16, 2, 64, PC), BF)
    return pl.pallas_call(
        pack_kernel,
        out_shape=(
            jax.ShapeDtypeStruct((16, 192, NB), BF), t, t, t,
            jax.ShapeDtypeStruct((INTS,), jnp.int32), jax.ShapeDtypeStruct((FLOATS,), F32),
        ),
        in_specs=[vm(), sm(), sm(), sm()],
        out_specs=(vm(), vm(), vm(), vm(), sm(), sm()),
        scratch_shapes=[
            pltpu.SMEM((SLOTS,), jnp.int32),
            pltpu.SMEM((2 * SLOTS,), jnp.int32),
            pltpu.SMEM((KIDS // 2,), jnp.int32),
            pltpu.SMEM((KIDS,), jnp.int32),
            pltpu.SMEM((2 * SLOTS,), jnp.int32),
        ],
        compiler_params=pltpu.CompilerParams(vmem_limit_bytes=24 << 20),
        name="pack",
    )(x, child_map, child_parent, pivot_order)


def factor_block(m_ref, inv_ref, hook):
    rid = lax.broadcasted_iota(jnp.int32, (8, 1), 0)
    rows = [m_ref[8 * r : 8 * r + 8, :] for r in range(16)]
    for q in range(16):
        if q == 5:
            hook()
        c0 = 8 * q
        rb = [jnp.broadcast_to(rows[q][s : s + 1, :], (8, 2 * NB)) for s in range(8)]
        e = [
            [
                jnp.broadcast_to(rb[s][:, c0 + t : c0 + t + 1], (8, NB)) if t >= s else None
                for t in range(8)
            ]
            for s in range(8)
        ]
        inv = [None] * 8
        for t in range(8):
            inv[t] = 1.0 / e[t][t]
            for s in range(t + 1, 8):
                m = e[t][s] * inv[t]
                for u in range(s, 8):
                    e[s][u] = e[s][u] - m * e[t][u]
                rb[s] = rb[s] - jnp.concatenate([m, m], 1) * rb[t]
        new, iv = rb[7], inv[7]
        for s in range(6, -1, -1):
            new = jnp.where(rid == s, rb[s], new)
            iv = jnp.where(rid == s, inv[s], iv)
        m_ref[c0 : c0 + 8, :] = new
        inv_ref[c0 : c0 + 8, :] = iv
        if q < 15:
            cols = jnp.transpose(new[:, :NB] * iv)
            for r in range(q + 1, 16):
                p = [cols[8 * r : 8 * r + 8, t : t + 1] * rb[t] for t in range(8)]
                rows[r] = rows[r] - (
                    ((p[0] + p[1]) + (p[2] + p[3])) + ((p[4] + p[5]) + (p[6] + p[7]))
                )


class Gather:
    def __init__(self, own, out, send, recv, rows):
        self.own, self.out, self.send, self.recv, self.half = own, out, send, recv, rows // 2
        self.f = lax.axis_index("front")
        g = lax.axis_index("grid")
        self.x, self.y = g // 4, g % 4

    def dev(self, axis, d):
        if axis == 0:
            return (self.f, lax.rem(self.x + d, 4) * 4 + self.y)
        return (self.f, self.x * 4 + lax.rem(self.y + d, 4))

    def at(self, axis, d, r0, rn):
        x, y = self.x, self.y
        if axis == 0:
            x = lax.rem(x + d, 4)
        else:
            y = lax.rem(y + d, 4)
        return self.out.at[x, y, pl.ds(r0, rn), :]

    def line(self, axis, d, r0, rn):
        if axis == 0:
            return self.out.at[lax.rem(self.x + d, 4), :, pl.ds(r0, rn), :]
        return self.out.at[:, lax.rem(self.y + d, 4), pl.ds(r0, rn), :]

    def copy(self, src, dst, sem, axis, d):
        return pltpu.make_async_remote_copy(
            src_ref=src,
            dst_ref=dst,
            send_sem=self.send.at[sem],
            recv_sem=self.recv.at[sem],
            device_id=self.dev(axis, d),
            device_id_type=MESH,
        )

    def stage(self, n):
        h = self.half
        q = h // 2
        out = []
        for axis in range(2):
            r0 = axis * h
            other = 1 - axis
            b = axis * 8
            if n == 0:
                src = self.own.at[pl.ds(r0, h), :]
                for i, d in enumerate((1, 3, 2)):
                    out.append(self.copy(src, self.at(axis, 0, r0, h), b + i, axis, d))
            elif n == 1:
                a = self.line(other, 0, r0, h)
                out.append(self.copy(a, a, b + 3, other, 1))
                out.append(self.copy(a, a, b + 4, other, 3))
            else:
                a = self.line(other, 3, r0, q)
                out.append(self.copy(a, a, b + 5, other, 1))
                a = self.line(other, 1, r0 + q, q)
                out.append(self.copy(a, a, b + 6, other, 3))
        return out

    def start(self, n):
        for c in self.stage(n):
            c.start()

    def wait_recv(self, n):
        for c in self.stage(n):
            c.wait_recv()

    def wait_send(self):
        for n in range(3):
            for c in self.stage(n):
                c.wait_send()


class Swap:
    def __init__(self, axis, src, dst, send, recv, local):
        f, g = lax.axis_index("front"), lax.axis_index("grid")
        self.axis, self.f, self.g = axis, f, g
        self.me = g if axis == "grid" else f
        self.src, self.dst, self.send, self.recv, self.local = src, dst, send, recv, local

    def copy(self, i):
        if self.axis == "grid":
            to = lax.rem(self.g // 4 + i // 4, 4) * 4 + lax.rem(self.g % 4 + i % 4, 4)
            dev = (self.f, to)
        else:
            to = lax.rem(self.f // 2 + i // 2, 8) * 2 + lax.rem(self.f % 2 + i % 2, 2)
            dev = (to, self.g)
        return pltpu.make_async_remote_copy(
            src_ref=self.src.at[to],
            dst_ref=self.dst(self.me),
            send_sem=self.send.at[i],
            recv_sem=self.recv.at[i],
            device_id=dev,
            device_id_type=MESH,
        )

    def keep(self):
        return pltpu.make_async_copy(self.src.at[self.me], self.dst(self.me), self.local)

    def start(self):
        def one(i, c):
            self.copy(i).start()
            return c

        lax.fori_loop(1, 16, one, 0)
        self.keep().start()

    def wait_recv(self):
        def one(i, c):
            self.copy(i).wait_recv()
            return c

        lax.fori_loop(1, 16, one, 0)
        self.keep().wait()

    def wait_send(self):
        def one(i, c):
            self.copy(i).wait_send()
            return c

        lax.fori_loop(1, 16, one, 0)


def main_kernel(
    ps1, a0, a1, a2, od_ref, or_ref, ints, floats,
    ud_ref, ur_ref, s_ref, sg_ref, acc_ref, end_ref,
    pr1, ps2, pr2, b0, b1, b2, c0, c1, c2, dsnd, psnd,
    w, m_ref, inv_ref, uh, ul, st, dall, tin, sv,
    asend, arecv, dsend, drecv, ssend, srecv, lsem, ksem, vsem,
):
    f = lax.axis_index("front")
    g = lax.axis_index("grid")
    x, y = g // 4, g % 4
    barrier = pltpu.get_barrier_semaphore()

    def greet(i, c):
        to = lax.rem(g + i, 16)
        pl.semaphore_signal(barrier, inc=1, device_id=(f, to), device_id_type=MESH)
        to = lax.rem(f + i, 16)
        pl.semaphore_signal(barrier, inc=1, device_id=(to, g), device_id_type=MESH)
        return c

    lax.fori_loop(1, 16, greet, 0)

    def swap(n, axis, src, dst):
        return Swap(axis, src, dst, asend.at[n], arecv.at[n], ksem.at[n])

    lane = lax.broadcasted_iota(jnp.int32, (192, NB), 1)

    panel1 = swap(0, "grid", ps1, lambda me: pr1.at[me])
    panel2 = swap(1, "front", ps2, lambda me: pr2.at[pl.ds(3 * me, 3)])
    pswap = swap(2, "grid", psnd, lambda me: w.at[pl.ds(64 * me, 64), pl.ds(N, PC)])

    def trail1(s):
        dst = (b0, b1, b2)[s]
        return swap(3 + s, "grid", (a0, a1, a2)[s], lambda me: dst.at[pl.ds(2 * me, 2)])

    def trail2(s):
        return swap(6 + s, "front", (c0, c1, c2)[s], lambda me: tin.at[3 * me + s])

    pl.semaphore_wait(barrier, 30)
    panel1.start()

    trail1(0).start()
    trail1(1).start()
    panel1.wait_recv()

    def sort_panel(p, carry):
        x0 = pr1[ints[SOURCE + 2 * p]].astype(F32)
        x1 = pr1[ints[SOURCE + 2 * p + 1]].astype(F32)
        m0 = floats[2 * p]
        m1 = floats[2 * p + 1]
        x0 = x0 * (1.0 - m0) + pltpu.roll(x0, 64, 1) * m0
        x1 = x1 * m1 + pltpu.roll(x1, 64, 1) * (1.0 - m1)
        z = jnp.where(lane < 64, x0, x1).astype(BF)
        for v in range(3):
            ps2[p, v] = z[64 * v : 64 * v + 64]
        return carry

    lax.fori_loop(0, 16, sort_panel, 0)
    panel2.start()

    def sort_trail(s):
        trail1(s).wait_recv()
        src, dst = (b0, b1, b2)[s], (c0, c1, c2)[s]

        def one(p, carry):
            for t in range(2):
                dst[p, t] = src[ints[ORDER + 2 * p + t]]
            return carry

        lax.fori_loop(0, 16, one, 0)
        trail2(s).start()

    sort_trail(0)
    panel2.wait_recv()

    def pivot_rows(slot):
        halves = []
        for v in range(2):
            total = jnp.zeros((64, NB), F32)
            for t in range(2):
                z = pr2[ints[UNIT + 2 * (t * SLOTS + slot) + v]].astype(F32)
                if t == 1:
                    z = pltpu.roll(z, 64, 1)
                total = total + z * floats[HAS + t * SLOTS + slot]
            halves.append(total)
        return jnp.transpose(jnp.concatenate(halves, 0))[:64]

    for i in range(5):
        j = lax.rem(g // 2 + i, 8)
        od = od_ref[:, pl.ds(pl.multiple_of(j * NB, NB), NB)].astype(F32)
        dsnd[:, i * NB : (i + 1) * NB] = pivot_rows(j) + od
    gd = Gather(dsnd, dall, dsend, drecv, 64)
    gd.start(0)
    dall[x, y] = dsnd[...]

    def rest(m, carry):
        for i in range(3):
            psnd[m, :, i * NB : (i + 1) * NB] = pivot_rows(8 + 3 * m + i)
        return carry

    lax.fori_loop(0, 16, rest, 0)
    for n in range(2):
        gd.wait_recv(n)
        gd.start(n + 1)
    pswap.start()
    trail1(2).start()
    sort_trail(1)
    gd.wait_recv(2)

    def cyclic(r, i):
        return jnp.concatenate(
            [dall[b // 4, b % 4, :, i * NB : (i + 1) * NB] for b in (2 * r, 2 * r + 1)], 0
        )

    for r in range(8):
        for c in range(8):
            if c < r:
                z = jnp.zeros((NB, NB), F32)
            elif c - r <= 4:
                z = cyclic(r, c - r)
            else:
                z = jnp.transpose(cyclic(c, 8 - (c - r)))
            w[r * NB : (r + 1) * NB, c * NB : (c + 1) * NB] = z
    eye = (
        lax.broadcasted_iota(jnp.int32, (NB, NB), 0) == lax.broadcasted_iota(jnp.int32, (NB, NB), 1)
    ).astype(F32)

    def gs(k):
        return Gather(st.at[k], sg_ref.at[k], ssend.at[k], srecv.at[k], PC)

    def local(k):
        return pltpu.make_async_copy(st.at[k], sg_ref.at[k, x, y], lsem.at[k])

    def move(k, n):
        c = gs(k)
        c.wait_recv(n - 1)
        if n == 1:
            local(k).wait()
        c.start(n)

    def load(n):
        return pltpu.make_async_copy(sg_ref.at[pl.ds(2 * n, 2)], (sv, end_ref)[n % 2], vsem.at[n % 2])

    def fetch(n):
        for k in (2 * n, 2 * n + 1):
            gs(k).wait_recv(2)
        load(n).start()

    def product(n, m):
        lhs = jnp.concatenate([(sv, end_ref)[n % 2][k, m // 4, m % 4] for k in range(2)], 1)
        return dg(lhs, s_ref[2 * NB * n : 2 * NB * (n + 1), :], 1, 0)

    def step(k, carry):
        r0 = pl.multiple_of(k * NB, NB)
        m_ref[:, :NB] = w[pl.ds(r0, NB), pl.ds(r0, NB)]
        m_ref[:, NB:] = eye

        def hook():
            @pl.when(k >= 1)
            def _():
                move(k - 1, 1)

        factor_block(m_ref, inv_ref, hook)

        @pl.when(k == N // NB - 1)
        def _():
            fetch(0)
            fetch(1)

        @pl.when(k == 0)
        def _():
            pswap.wait_recv()
            w[:, N:] = w[:, N:] + or_ref[0].astype(F32)

        @pl.when(k == 3)
        def _():
            sort_trail(2)

        lh, ll = split(m_ref[:, NB:])
        ah, al = split(w[pl.ds(r0, NB), :])
        u = dg(lh, ah, 1, 0) + (dg(lh, al, 1, 0) + dg(ll, ah, 1, 0))
        w[pl.ds(r0, NB), :] = u
        h, l = split(u)
        uh[...] = h
        ul[...] = l
        iv = inv_ref[...]
        top = u[:, N:]
        ur_ref[pl.ds(r0, NB), :] = top
        rs = jnp.sqrt(iv)
        solved = top * jnp.concatenate([rs] * 3, 1)
        s_ref[pl.ds(r0, NB), :] = solved.astype(BF)
        st[k] = jnp.transpose(solved).astype(BF)
        gs(k).start(0)
        local(k).start()

        def upd(i, c):
            i0 = pl.multiple_of(i * NB, NB)
            xh, xl = split((uh[:, pl.ds(i0, NB)].astype(F32) + ul[:, pl.ds(i0, NB)].astype(F32)) * iv)
            d = dg(xh, uh[...], 0, 0) + (dg(xh, ul[...], 0, 0) + dg(xl, uh[...], 0, 0))
            w[pl.ds(i0, NB), :] = w[pl.ds(i0, NB), :] - d
            return c

        lax.fori_loop(k + 1, N // NB, upd, 0)

        @pl.when(k >= 1)
        def _():
            move(k - 1, 2)

        return carry

    last = N // NB - 1
    lax.fori_loop(0, N // NB, step, 0)
    load(0).wait()

    def first(m, c):
        acc_ref[pl.ds(pl.multiple_of(m * PC, PC), PC), :] = product(0, m)
        return c

    lax.fori_loop(0, 16, first, 0)
    fetch(2)
    move(last, 1)
    load(1).wait()

    def second(m, c):
        rows = pl.ds(pl.multiple_of(m * PC, PC), PC)
        acc_ref[rows, :] = acc_ref[rows, :] + product(1, m)
        return c

    lax.fori_loop(0, 16, second, 0)
    move(last, 2)
    blk = pl.multiple_of((g // 2) * NB, NB)
    col = 64 * g + lax.broadcasted_iota(jnp.int32, (64, NB), 0)
    for r in range(8):
        own = jnp.transpose(w[r * NB : (r + 1) * NB, pl.ds(blk, NB)])
        own = jnp.where(g % 2 == 1, own[64:], own[:64])
        row = r * NB + lax.broadcasted_iota(jnp.int32, (64, NB), 1)
        ud_ref[:, r * NB : (r + 1) * NB] = jnp.where(row <= col, own, 0.0)
    for s in range(3):
        trail1(s).wait_send()
        trail2(s).wait_send()
        trail2(s).wait_recv()
    load(2).wait()

    def third(m, c):
        for i in range(3):
            for v in range(2):
                r = i * NB + v * 64
                total = jnp.zeros((64, PC), F32)
                for t in range(2):
                    e = t * SLOTS + 8 + 3 * m + i
                    total = total + tin[ints[UNIT + 2 * e + v], t].astype(F32) * floats[HAS + e]
                rows = pl.ds(pl.multiple_of(m * PC + r, 64), 64)
                acc_ref[rows, :] = total - acc_ref[rows, :]
        rows = pl.ds(pl.multiple_of(m * PC, PC), PC)
        acc_ref[rows, :] = acc_ref[rows, :] - product(2, m)
        return c

    lax.fori_loop(0, 16, third, 0)
    for e in (panel1, panel2, pswap):
        e.wait_send()
    gd.wait_send()

    fetch(3)

    def finish(k, carry):
        gs(k).wait_send()
        return carry

    lax.fori_loop(0, N // NB, finish, 0)
    load(3).wait()


def main_call(ps1, a0, a1, a2, orig_diag, orig_rows, *tables):
    steps = N // NB
    hbm = pl.BlockSpec(memory_space=pl.ANY)
    panel = pltpu.VMEM((16, 192, NB), BF)
    send = pltpu.VMEM((16, 2, 64, PC), BF)
    recv = pltpu.VMEM((KIDS, 64, PC), BF)
    sems = pltpu.SemaphoreType.DMA
    return pl.pallas_call(
        main_kernel,
        out_shape=(
            jax.ShapeDtypeStruct((64, N), F32),
            jax.ShapeDtypeStruct((N, PC), F32),
            jax.ShapeDtypeStruct((N, PC), BF),
            jax.ShapeDtypeStruct((steps, 4, 4, PC, NB), BF),
            jax.ShapeDtypeStruct((16 * PC, PC), F32),
            jax.ShapeDtypeStruct((2, 4, 4, PC, NB), BF),
        ),
        in_specs=[vm(), vm(), vm(), vm(), vm(), vm(), sm(), sm()],
        out_specs=(vm(), vm(), vm(), hbm, vm(), vm()),
        scratch_shapes=[
            panel, pltpu.VMEM((16, 3, 64, NB), BF), pltpu.VMEM((48, 64, NB), BF),
            recv, recv, recv, send, send, send,
            pltpu.VMEM((64, PW), F32),
            pltpu.VMEM((16, 64, PC), F32),
            pltpu.VMEM((N, WT), F32),
            pltpu.VMEM((NB, 2 * NB), F32),
            pltpu.VMEM((NB, NB), F32),
            pltpu.VMEM((NB, WT), BF),
            pltpu.VMEM((NB, WT), BF),
            pltpu.VMEM((steps, PC, NB), BF),
            pltpu.VMEM((4, 4, 64, PW), F32),
            pltpu.VMEM((48, 2, 64, PC), BF),
            pltpu.VMEM((2, 4, 4, PC, NB), BF),
            sems((9, 16)), sems((9, 16)), sems((16,)), sems((16,)),
            sems((steps, 16)), sems((steps, 16)), sems((steps,)), sems((9,)), sems((2,)),
        ],
        compiler_params=pltpu.CompilerParams(
            vmem_limit_bytes=65 << 19, collective_id=0, has_side_effects=True
        ),
        name="assemble_factor_gather",
    )(ps1, a0, a1, a2, orig_diag, orig_rows, *tables)


def schur_kernel(end_ref, s_ref, acc_ref, ud_ref, ur_ref, o_ref, udo_ref, uro_ref):
    uro_ref[0] = ur_ref[...]
    udo_ref[...] = ud_ref[...]
    m = pl.program_id(0)
    for i in range(2):
        b = 2 * m + i
        lhs = jnp.concatenate([end_ref[k, b] for k in range(2)], 1)
        rows = pl.ds(pl.multiple_of(b * PC, PC), PC)
        o_ref[0, i * PC : (i + 1) * PC, :] = (
            acc_ref[rows, :] - dg(lhs, s_ref[6 * NB :, :], 1, 0)
        ).astype(BF)


def schur_call(end, s, acc, ud, ur):
    return pl.pallas_call(
        schur_kernel,
        out_shape=(
            jax.ShapeDtypeStruct((1, 16 * PC, PC), BF),
            jax.ShapeDtypeStruct((64, N), F32),
            jax.ShapeDtypeStruct((1, N, PC), F32),
        ),
        grid=(8,),
        in_specs=[
            vm(),
            vm(),
            vm(),
            pl.BlockSpec((64, NB), lambda m: (0, m)),
            pl.BlockSpec((NB, PC), lambda m: (m, 0)),
        ],
        out_specs=(
            pl.BlockSpec((1, 2 * PC, PC), lambda m: (0, m, 0)),
            pl.BlockSpec((64, NB), lambda m: (0, m)),
            pl.BlockSpec((1, NB, PC), lambda m: (0, m, 0)),
        ),
        compiler_params=pltpu.CompilerParams(vmem_limit_bytes=20 << 20),
        name="schur",
    )(end.reshape(2, 16, PC, NB), s, acc, ud, ur)


def shards(child_blocks, orig_diag, orig_rows, child_map, child_parent, pivot_order):
    panel, a0, a1, a2, ints, floats = pack(child_blocks, child_map, child_parent, pivot_order)
    upper_diag, upper_rows, s, _, acc, end = main_call(
        panel, a0, a1, a2, orig_diag[0].T, orig_rows, ints, floats
    )
    schur, upper_diag, upper_rows = schur_call(end, s, acc, upper_diag, upper_rows)
    return upper_diag.T[None], upper_rows, schur


def solution(mesh):
    return jax.shard_map(
        shards,
        mesh=mesh,
        in_specs=(
            P("grid", "front", None),
            P("front", None, "grid"),
            P("front", None, "grid"),
            P(),
            P(),
            P(),
        ),
        out_specs=(P("front", None, "grid"), P("front", None, "grid"), P("front", None, "grid")),
        check_vma=False,
    )
```
